32 devices in a mesh: rep: 4 (over x, core), row: 4 (over z), col: 2 (over y).
Axes of the slice: x: 2, y: 2, z: 4, core: 2. Of those that a mesh axis runs over, the one named last changes fastest.
Arguments:
- inputs: bfloat16 [4, 128, 6144], P('rep', 'col', 'row'), may hold values from -6 to 6
- w_in: bfloat16 [6144, 24576], P('row', ('rep', 'col')), may hold values from -0.078125 to 0.078125
- w_out: bfloat16 [24576, 6144], P(('rep', 'col'), 'row'), may hold values from -0.0390625 to 0.0390625
- cotangent: bfloat16 [4, 128, 6144], P('rep', 'col', 'row'), may hold values from -1536 to 1536
- counts: int32 [4], replicated, may hold values from 0 to 4, as said below
Outputs:
- block_output: bfloat16 [4, 128, 6144], P('rep', 'col', 'row')
- input_grad: bfloat16 [4, 128, 6144], P('rep', 'col', 'row')
- w_in_grad: float32 [6144, 24576], P('row', ('rep', 'col'))
- w_out_grad: float32 [24576, 6144], P(('rep', 'col'), 'row')
The draws below stay inside these ranges and needn't reach their ends.
Inputs may be any that keep to these rules, and one draw needn't show every extreme that they name: Replica r completed its first counts[r] micro-batches; at least one replica completed all 4.
All inputs are finite; a program needn't handle non-finite values.
Results may differ from the reference program's by a relative error of at most 0.015.
Values may be sent and summed in bfloat16 or wider, within the bound.
A program may use at most 192 MiB of HBM per device.

```python
import jax
import jax.numpy as jnp

D = 6144
FF = 24576
MB = 4
MBT = 32
TOKENS = 128
N_REP = 4
N_ROW = 4
N_COL = 2


def draw_counts(key, part):
    first = jax.random.fold_in(key, 11)
    second = jax.random.fold_in(key, 23)
    values = jax.random.randint(first, (N_REP,), 0, MB + 1)
    chosen = jax.random.randint(second, (), 0, N_REP)
    return jnp.where(jnp.arange(N_REP) == chosen, MB, values).astype(jnp.int32)


def block_scale(stream_key, dims, cuts, least, top_value):
    level, own = 1.0, jax.random.fold_in(stream_key, 6)
    for axis_at, blocks in cuts:
        steps = jnp.exp(jax.random.uniform(jax.random.fold_in(own, axis_at), (blocks,), jnp.float32, least / len(cuts), top_value / len(cuts)))
        level = level * jnp.repeat(steps, dims[axis_at] // blocks).reshape([-1 if axis == axis_at else 1 for axis in range(len(dims))])
    return level


def noise(rng, dims, spread, most, shards=(), held_as=jnp.bfloat16):
    array = jax.random.normal(rng, dims, jnp.float32) * spread
    if len(shards) > 0:
        array = block_scale(rng, dims, shards, -0.22, 0.18) * array
    return jnp.clip(array, min=-most, max=most).astype(held_as)


def setup_inputs(seed: int = 0) -> dict:
    streams_of = jax.random.split(jax.random.key(seed), 6)
    return {
        "inputs": noise(streams_of[0], (N_REP, TOKENS, D), 1.0, 6.0, ((0, 4), (1, 2), (2, 4))),
        "w_in": noise(streams_of[1], (D, FF), D ** -0.5, 0.078125, ((0, 4), (1, 8))),
        "w_out": noise(streams_of[2], (FF, D), FF ** -0.5, 0.0390625, ((0, 8), (1, 4))),
        "cotangent": noise(streams_of[3], (N_REP, TOKENS, D), (MBT * MB * N_REP // 2), 1536.0, ((0, 4), (1, 2), (2, 4))),
        "counts": draw_counts(jax.random.fold_in(streams_of[5], 71), 0),
    }


root_coef = 0.7978845608028654
cubic_coef = 0.044715


def gelu_tanh(values):
    inner = root_coef * (values + cubic_coef * values * values * values)
    return 0.5 * values * (1.0 + jnp.tanh(inner))


def gelu_slope(values):
    inner = root_coef * (values + cubic_coef * values * values * values)
    tangent = jnp.tanh(inner)
    return 0.5 * (1.0 + tangent) + 0.5 * values * (1.0 - tangent * tangent) * root_coef * (1.0 + 3.0 * cubic_coef * values * values)


def rounded_term(left, right):
    return jnp.dot(left, right, preferred_element_type=jnp.float32).astype(jnp.bfloat16).astype(jnp.float32)


def block_sum(left, right):
    width = left.shape[1] // N_ROW
    total = jnp.zeros((left.shape[0], right.shape[1]), jnp.float32)
    for block in range(N_ROW):
        total = total + rounded_term(left[:, block * width:(block + 1) * width], right[block * width:(block + 1) * width, :])
    return total


def set_sum(left, right):
    piece = FF // (N_REP * N_COL)
    left_sets = left.reshape(left.shape[0], N_REP, N_COL, piece)
    right_sets = right.reshape(N_REP, N_COL, piece, right.shape[1])
    total = jnp.zeros((left.shape[0], right.shape[1]), jnp.float32)
    for group in range(N_COL):
        left_part = left_sets[:, :, group, :].reshape(left.shape[0], N_REP * piece)
        right_part = right_sets[:, group, :, :].reshape(N_REP * piece, right.shape[1])
        total = total + rounded_term(left_part, right_part)
    return total


def reference(inputs, w_in, w_out, cotangent, counts):
    token_total = (MBT * jnp.sum(counts)).astype(jnp.float32)
    positions = jnp.arange(MB * MBT, dtype=jnp.int32)
    outputs = []
    grads = []
    w_in_grad = jnp.zeros((D, FF), jnp.float32)
    w_out_grad = jnp.zeros((FF, D), jnp.float32)
    w_out_t = w_out.T
    w_in_t = w_in.T
    for replica in range(N_REP):
        tokens = inputs[replica]
        kept_mask = (positions // MBT < counts[replica]).astype(jnp.float32)
        hidden = block_sum(tokens, w_in)
        activated = gelu_tanh(hidden).astype(jnp.bfloat16)
        mixed = set_sum(activated, w_out)
        outputs.append((tokens.astype(jnp.float32) + mixed).astype(jnp.bfloat16))
        scaled = (cotangent[replica].astype(jnp.float32) * kept_mask[:, None] / token_total).astype(jnp.bfloat16)
        slope_sum = block_sum(scaled, w_out_t)
        hidden_grad = (slope_sum * gelu_slope(hidden)).astype(jnp.bfloat16)
        back = set_sum(hidden_grad, w_in_t)
        grads.append((scaled.astype(jnp.float32) + back).astype(jnp.bfloat16))
        w_in_grad = w_in_grad + jnp.dot(tokens.T, hidden_grad, preferred_element_type=jnp.float32)
        w_out_grad = w_out_grad + jnp.dot(activated.T, scaled, preferred_element_type=jnp.float32)
    return (jnp.stack(outputs), jnp.stack(grads), w_in_grad, w_out_grad)
```

```python
import functools

import jax
import jax.numpy as jnp
from jax import lax
from jax.experimental import pallas as pl
from jax.experimental.pallas import tpu as pltpu
from jax.sharding import PartitionSpec as P

MBT = 32
HALF = 128
GROUP = 2 * HALF
LAG = 2
MESH = pl.DeviceIdType.MESH

root_coef = 0.7978845608028654
cubic_coef = 0.044715


def gelu_tanh(values):
    inner = root_coef * (values + cubic_coef * values * values * values)
    return 0.5 * values * (1.0 + jnp.tanh(inner))


def gelu_slope(values):
    inner = root_coef * (values + cubic_coef * values * values * values)
    tangent = jnp.tanh(inner)
    return 0.5 * (1.0 + tangent) + 0.5 * values * (1.0 - tangent * tangent) * root_coef * (
        1.0 + 3.0 * cubic_coef * values * values
    )


def wide(values):
    return values.astype(jnp.float32)


def narrow(values):
    return values.astype(jnp.bfloat16)


def product(left, right):
    return jnp.dot(left, right, preferred_element_type=jnp.float32)


def right_product(left, right):
    return lax.dot_general(
        left, right, (((1,), (1,)), ((), ())), preferred_element_type=jnp.float32
    )


def first_product(left, right):
    return lax.dot_general(
        left, right, (((0,), (0,)), ((), ())), preferred_element_type=jnp.float32
    )


def rows_at(start, size):
    return pl.ds(pl.multiple_of(start, size), size)


def step_kernel(
    sizes,
    counts, x_ref, cot_ref, w1_hbm, w2_hbm,
    bo_ref, ig_ref, act_hbm, grad_hbm, xa_hbm, sa_hbm,
    w1, w2, xa, sa, scaled,
    part, came, result,
    acc, pair_out, pair_in, chip_out, chip_in,
    w_sem, near_send, near_recv, pair_send, pair_recv,
    part_send, part_recv, res_send, res_recv, out_sem,
    pair2_send, pair2_recv, chip_send, chip_recv,
):
    n_rep, n_row, n_col, tl, width, hidden, groups = sizes
    total_rows = n_rep * n_col * tl
    halves = hidden // HALF
    rep, row, col = (lax.axis_index(name) for name in ("rep", "row", "col"))
    core, chip = lax.rem(rep, 2), rep // 2
    n_chip = n_rep // 2
    partner = rep + 1 - 2 * core
    block = rep * n_col + col
    offsets = [(i, j) for i in range(n_chip) for j in range(n_col) if i + j > 0]
    near = len(offsets)

    def to_of(i, j):
        return lax.rem(chip + i, n_chip), lax.rem(col + j, n_col)

    def from_of(i, j):
        return lax.rem(chip + n_chip - i, n_chip), lax.rem(col + n_col - j, n_col)

    def block_rows(chip_at, core_at, col_at):
        return rows_at(((2 * chip_at + core_at) * n_col + col_at) * tl, tl)

    def each(count, body):
        lax.fori_loop(0, count, lambda i, c: (body(i), c)[1], 0)

    def size_of(i):
        return min(GROUP, hidden - i * GROUP)

    def w1_copy(i):
        return pltpu.make_async_copy(
            w1_hbm.at[:, pl.ds(i * GROUP, size_of(i))],
            w1.at[i, :, pl.ds(0, size_of(i))],
            w_sem.at[0, i],
        )

    def w2_copy(i):
        return pltpu.make_async_copy(
            w2_hbm.at[pl.ds(i * GROUP, size_of(i)), :],
            w2.at[i, pl.ds(0, size_of(i)), :],
            w_sem.at[1, i],
        )

    for i in range(groups):
        if size_of(i) < GROUP:
            w1[i, :, size_of(i):] = jnp.zeros((width, GROUP - size_of(i)), jnp.bfloat16)
            w2[i, size_of(i):, :] = jnp.zeros((GROUP - size_of(i), width), jnp.bfloat16)
        w1_copy(i).start()
    for i in range(groups):
        w2_copy(i).start()

    barrier = pltpu.get_barrier_semaphore()
    for i, j in offsets:
        chip_at, col_at = to_of(i, j)
        pl.semaphore_signal(
            barrier, inc=1, device_id=(2 * chip_at + core, row, col_at), device_id_type=MESH
        )
    pl.semaphore_signal(barrier, inc=1, device_id=(partner, row, col), device_id_type=MESH)

    @pl.when(row > 0)
    def _():
        pl.semaphore_signal(barrier, inc=1, device_id=(rep, row - 1, col), device_id_type=MESH)

    @pl.when(row < n_row - 1)
    def _():
        pl.semaphore_signal(barrier, inc=1, device_id=(rep, row + 1, col), device_id_type=MESH)

    at_ends = jnp.where(row > 0, 1, 0) + jnp.where(row < n_row - 1, 1, 0)
    pl.semaphore_wait(barrier, near + 1 + at_ends)

    def near_copy(which, source, target, k):
        i, j = offsets[k]
        chip_at, col_at = to_of(i, j)
        return pltpu.make_async_remote_copy(
            src_ref=source,
            dst_ref=target.at[block_rows(chip, core, col), :],
            send_sem=near_send.at[which, k],
            recv_sem=near_recv.at[which, k],
            device_id=(2 * chip_at + core, row, col_at),
            device_id_type=MESH,
        )

    def pair_copy(which, source, target, k):
        rows = block_rows(chip, core, col)
        if k < near:
            chip_at, col_at = from_of(*offsets[k])
            rows = block_rows(chip_at, core, col_at)
            source = target.at[rows, :]
        return pltpu.make_async_remote_copy(
            src_ref=source,
            dst_ref=target.at[rows, :],
            send_sem=pair_send.at[which, k],
            recv_sem=pair_recv.at[which, k],
            device_id=(partner, row, col),
            device_id_type=MESH,
        )

    def gather_start(which, source, target):
        for k in range(near):
            near_copy(which, source, target, k).start()
        pair_copy(which, source, target, near).start()

    def gather_pass(which, source, target):
        for k in range(near):
            near_copy(which, source, target, k).wait_recv()
            pair_copy(which, source, target, k).start()

    def gather_end(which, source, target):
        for k in range(near + 1):
            pair_copy(which, source, target, k).wait_recv()

    gather_start(0, x_ref, xa)
    own = block_rows(chip, core, col)
    xa[own, :] = x_ref[...]
    kept_rows = MBT * counts[rep]
    counted = counts[0]
    for r in range(1, n_rep):
        counted = counted + counts[r]
    token_total = (MBT * counted).astype(jnp.float32)
    position = col * tl + lax.broadcasted_iota(jnp.int32, (tl, width), 0)
    kept = jnp.where(position < kept_rows, 1.0, 0.0)
    value = narrow(wide(cot_ref[...]) * kept / token_total)
    scaled[...] = value
    sa[own, :] = value
    gather_pass(0, x_ref, xa)
    gather_start(1, scaled, sa)
    gather_end(0, x_ref, xa)

    kinds = 2
    result_tick = max(kinds * groups, (n_row - 1) * LAG + 1)
    use_tick = result_tick + (n_row - 1) * LAG
    ticks = use_tick + kinds * groups
    places = (row, n_row - 1 - row)
    nexts = (row + 1, row - 1)

    def part_copy(kind, i, d):
        return pltpu.make_async_remote_copy(
            src_ref=part.at[kind, i, d],
            dst_ref=came.at[kind, i, d],
            send_sem=part_send.at[kind, i, d],
            recv_sem=part_recv.at[kind, i, d],
            device_id=(rep, nexts[d], col),
            device_id_type=MESH,
        )

    def result_copy(kind, i, d):
        return pltpu.make_async_remote_copy(
            src_ref=result.at[kind, i, 1 - d],
            dst_ref=result.at[kind, i, 1 - d],
            send_sem=res_send.at[kind, i, d],
            recv_sem=res_recv.at[kind, i, d],
            device_id=(rep, nexts[d], col),
            device_id_type=MESH,
        )

    def out_copy(kind, i, h):
        target = (act_hbm, grad_hbm)[kind]
        return pltpu.make_async_copy(
            result.at[kind, i, h],
            target.at[:, pl.ds(pl.multiple_of(i * GROUP + h * HALF, HALF), HALF)],
            out_sem.at[kind, i, h],
        )

    def make_part(kind, i):
        if kind == 0:
            value = product(xa[...], w1[i])
        else:
            value = right_product(sa[...], w2[i])
        value = narrow(value)
        part[kind, i, 0] = value[:, :HALF]
        part[kind, i, 1] = value[:, HALF:]

    def finish(kind, i, d):
        total = wide(part[0, i, d]) + wide(came[0, i, d])
        if kind == 0:
            result[0, i, d] = narrow(gelu_tanh(total))
        else:
            slope = wide(part[1, i, d]) + wide(came[1, i, d])
            result[1, i, d] = narrow(slope * gelu_slope(total))

    def add_up(kind, i):
        left = jnp.concatenate([result[kind, i, 0], result[kind, i, 1]], axis=1)

        def strip(n):
            columns = rows_at(n * GROUP, GROUP)
            if kind == 0:
                more = product(left, w2[i, :, columns])
            else:
                more = right_product(left, w1[i, columns, :])

            @pl.when(i == 0)
            def _():
                acc[kind, :, columns] = more

            @pl.when(i > 0)
            def _():
                acc[kind, :, columns] = acc[kind, :, columns] + more

        each(width // GROUP, strip)

    def tick_part(kind, d, i):
        place = places[d]

        @pl.when(place > 0)
        def _():
            part_copy(kind, i, d).wait_recv()

        @pl.when(jnp.logical_and(place > 0, place < n_row - 1))
        def _():
            part[kind, i, d] = narrow(wide(part[kind, i, d]) + wide(came[kind, i, d]))

        @pl.when(place < n_row - 1)
        def _():
            part_copy(kind, i, d).start()

        @pl.when(place == n_row - 1)
        def _():
            finish(kind, i, d)

    def tick_result(kind, d, i):
        @pl.when(places[d] > 0)
        def _():
            result_copy(kind, i, d).wait_recv()

        @pl.when(places[d] < n_row - 1)
        def _():
            result_copy(kind, i, d).start()

    def pair2_copy(kind):
        return pltpu.make_async_remote_copy(
            src_ref=pair_out.at[kind],
            dst_ref=pair_in.at[kind],
            send_sem=pair2_send.at[kind],
            recv_sem=pair2_recv.at[kind],
            device_id=(partner, row, col),
            device_id_type=MESH,
        )

    def chip_copy(kind, k):
        chip_at, col_at = to_of(*offsets[k])
        return pltpu.make_async_remote_copy(
            src_ref=chip_out.at[kind, k],
            dst_ref=chip_in.at[kind, k],
            send_sem=chip_send.at[kind, k],
            recv_sem=chip_recv.at[kind, k],
            device_id=(2 * chip_at + core, row, col_at),
            device_id_type=MESH,
        )

    def sum_start(kind):
        for k in range(n_chip * n_col):
            rows = block_rows(k // n_col, 1 - core, k % n_col)
            pair_out[kind, k * tl:(k + 1) * tl, :] = narrow(acc[kind, rows, :])
        pair2_copy(kind).start()

    def both_cores(kind, chip_at, col_at):
        theirs = pair_in[kind, rows_at((chip_at * n_col + col_at) * tl, tl), :]
        return acc[kind, block_rows(chip_at, core, col_at), :] + wide(theirs)

    def sum_pass(kind):
        pair2_copy(kind).wait_recv()
        for k in range(near):
            chip_out[kind, k] = narrow(both_cores(kind, *to_of(*offsets[k])))
            chip_copy(kind, k).start()

    def sum_end(kind, target, base):
        total = both_cores(kind, chip, col)
        for k in range(near):
            chip_copy(kind, k).wait_recv()
            total = total + wide(chip_in[kind, k])
        target[...] = narrow(wide(base[...]) + total)

    def out_start(kind, i):
        for h in range(2):
            @pl.when(2 * i + h < halves)
            def _():
                out_copy(kind, i, h).start()

    xa_out = pltpu.make_async_copy(xa, xa_hbm, out_sem.at[0, groups, 0])
    sa_out = pltpu.make_async_copy(sa, sa_hbm, out_sem.at[0, groups, 1])

    for i in range(groups):
        w1_copy(i).wait()
    xa_out.start()
    make_part(0, 0)

    def tick(t):
        for d in range(2):
            m = t - places[d] * LAG
            for kind in range(kinds):
                i = m - kind * groups

                @pl.when(jnp.logical_and(i >= 0, i < groups))
                def _():
                    tick_part(kind, d, i)

            for kind in range(kinds):
                j = m - result_tick - kind * groups

                @pl.when(jnp.logical_and(j >= 0, j < groups))
                def _():
                    tick_result(kind, d, j)

        ahead = t + 1

        @pl.when(ahead < groups)
        def _():
            make_part(0, ahead)

        @pl.when(ahead == groups)
        def _():
            gather_end(1, scaled, sa)
            for i in range(groups):
                w2_copy(i).wait()
            sa_out.start()

        @pl.when(jnp.logical_and(ahead >= groups, ahead < 2 * groups))
        def _():
            make_part(1, ahead - groups)

        @pl.when(t == min(3, groups - 1))
        def _():
            gather_pass(1, scaled, sa)

        for kind in range(kinds):
            i = t - use_tick - kind * groups

            @pl.when(jnp.logical_and(i >= 0, i < groups))
            def _():
                out_start(kind, i)
                add_up(kind, i)

        @pl.when(t == use_tick + groups)
        def _():
            sum_start(0)

        @pl.when(t == use_tick + groups + 1)
        def _():
            sum_pass(0)

    each(ticks, tick)
    sum_start(1)
    sum_end(0, bo_ref, x_ref)
    sum_pass(1)
    sum_end(1, ig_ref, scaled)

    for which, source, target in ((0, x_ref, xa), (1, scaled, sa)):
        for k in range(near):
            near_copy(which, source, target, k).wait_send()
        for k in range(near + 1):
            pair_copy(which, source, target, k).wait_send()
    for kind in range(kinds):
        pair2_copy(kind).wait_send()
        for k in range(near):
            chip_copy(kind, k).wait_send()
    xa_out.wait()
    sa_out.wait()

    def drain(i):
        for kind in range(kinds):
            for d in range(2):
                @pl.when(places[d] < n_row - 1)
                def _():
                    part_copy(kind, i, d).wait_send()
                    result_copy(kind, i, d).wait_send()

                @pl.when(2 * i + d < halves)
                def _():
                    out_copy(kind, i, d).wait()

    each(groups, drain)


def weight_grad(left, right, strip):
    rows, depth = left.shape[1], left.shape[0]
    columns = right.shape[1]

    def kernel(left_ref, right_ref, out_ref):
        out_ref[...] = first_product(left_ref[...], right_ref[...])

    return pl.pallas_call(
        kernel,
        grid=(rows // strip,),
        in_specs=[
            pl.BlockSpec((depth, strip), lambda i: (0, i)),
            pl.BlockSpec((depth, columns), lambda i: (0, 0), pipeline_mode=pl.Buffered(1)),
        ],
        out_specs=pl.BlockSpec((strip, columns), lambda i: (i, 0)),
        out_shape=jax.ShapeDtypeStruct((rows, columns), jnp.float32),
        cost_estimate=pl.CostEstimate(
            flops=2 * rows * depth * columns,
            bytes_accessed=4 * rows * columns + 2 * depth * (rows + columns),
            transcendentals=0,
        ),
    )(left, right)


def strip_of(size):
    return 256 if size % 256 == 0 else 128


def body(inputs, w_in, w_out, cotangent, counts):
    tl, width = inputs.shape[1], inputs.shape[2]
    hidden = w_in.shape[1]
    n_rep, n_row, n_col = (lax.axis_size(name) for name in ("rep", "row", "col"))
    groups = -(-hidden // GROUP)
    rows = n_rep * n_col * tl
    blocks = n_rep * n_col // 2
    near = blocks - 1
    sizes = (n_rep, n_row, n_col, tl, width, hidden, groups)
    bf16, f32 = jnp.bfloat16, jnp.float32
    vmem = pl.BlockSpec(memory_space=pltpu.VMEM)
    anyw = pl.BlockSpec(memory_space=pl.ANY)
    dma = pltpu.SemaphoreType.DMA
    block_output, input_grad, activated, hidden_grad, tokens_all, scaled_all = pl.pallas_call(
        functools.partial(step_kernel, sizes),
        out_shape=(
            jax.ShapeDtypeStruct((tl, width), bf16),
            jax.ShapeDtypeStruct((tl, width), bf16),
            jax.ShapeDtypeStruct((rows, hidden), bf16),
            jax.ShapeDtypeStruct((rows, hidden), bf16),
            jax.ShapeDtypeStruct((rows, width), bf16),
            jax.ShapeDtypeStruct((rows, width), bf16),
        ),
        in_specs=[pl.BlockSpec(memory_space=pltpu.SMEM), vmem, vmem, anyw, anyw],
        out_specs=(vmem, vmem, anyw, anyw, anyw, anyw),
        scratch_shapes=[
            pltpu.VMEM((groups, width, GROUP), bf16),
            pltpu.VMEM((groups, GROUP, width), bf16),
            pltpu.VMEM((rows, width), bf16),
            pltpu.VMEM((rows, width), bf16),
            pltpu.VMEM((tl, width), bf16),
            pltpu.VMEM((2, groups, 2, rows, HALF), bf16),
            pltpu.VMEM((2, groups, 2, rows, HALF), bf16),
            pltpu.VMEM((2, groups, 2, rows, HALF), bf16),
            pltpu.VMEM((2, rows, width), f32),
            pltpu.VMEM((2, blocks * tl, width), bf16),
            pltpu.VMEM((2, blocks * tl, width), bf16),
            pltpu.VMEM((2, near, tl, width), bf16),
            pltpu.VMEM((2, near, tl, width), bf16),
            dma((2, groups)),
            dma((2, near)),
            dma((2, near)),
            dma((2, near + 1)),
            dma((2, near + 1)),
            dma((2, groups, 2)),
            dma((2, groups, 2)),
            dma((2, groups, 2)),
            dma((2, groups, 2)),
            dma((2, groups + 1, 2)),
            dma((2,)),
            dma((2,)),
            dma((2, near)),
            dma((2, near)),
        ],
        compiler_params=pltpu.CompilerParams(
            collective_id=0, has_side_effects=True, vmem_limit_bytes=67_000_000
        ),
    )(
        counts,
        inputs.reshape(tl, width),
        cotangent.reshape(tl, width),
        w_in,
        w_out,
    )
    w_out_grad = weight_grad(activated, scaled_all, strip_of(hidden))
    w_in_grad = weight_grad(tokens_all, hidden_grad, strip_of(width))
    return (
        block_output.reshape(1, tl, width),
        input_grad.reshape(1, tl, width),
        w_in_grad,
        w_out_grad,
    )


def solution(mesh):
    placed = (
        P("rep", "col", "row"),
        P("row", ("rep", "col")),
        P(("rep", "col"), "row"),
        P("rep", "col", "row"),
        P(),
    )
    return jax.shard_map(
        body,
        mesh=mesh,
        in_specs=placed,
        out_specs=(
            P("rep", "col", "row"),
            P("rep", "col", "row"),
            P("row", ("rep", "col")),
            P(("rep", "col"), "row"),
        ),
        check_vma=False,
    )
```

```python
import functools

import jax
import jax.numpy as jnp
from jax import lax
from jax.experimental import pallas as pl
from jax.experimental.pallas import tpu as pltpu
from jax.sharding import PartitionSpec as P

MBT = 32
HALF = 128
GROUP = 2 * HALF
LAG = 3
SLOTS = 3
EIGHTHS = (4, 5, 6, 8)
MESH = pl.DeviceIdType.MESH

root_coef = 0.7978845608028654
cubic_coef = 0.044715


def gelu_tanh(values):
    inner = root_coef * (values + cubic_coef * values * values * values)
    return 0.5 * values * (1.0 + jnp.tanh(inner))


def gelu_slope(values):
    inner = root_coef * (values + cubic_coef * values * values * values)
    tangent = jnp.tanh(inner)
    return 0.5 * (1.0 + tangent) + 0.5 * values * (1.0 - tangent * tangent) * root_coef * (
        1.0 + 3.0 * cubic_coef * values * values
    )


def wide(values):
    return values.astype(jnp.float32)


def narrow(values):
    return values.astype(jnp.bfloat16)


def product(left, right):
    return jnp.dot(left, right, preferred_element_type=jnp.float32)


def right_product(left, right):
    return lax.dot_general(
        left, right, (((1,), (1,)), ((), ())), preferred_element_type=jnp.float32
    )


def first_product(left, right):
    return lax.dot_general(
        left, right, (((0,), (0,)), ((), ())), preferred_element_type=jnp.float32
    )


def rows_at(start, size):
    return pl.ds(pl.multiple_of(start, size), size)


def each(count, body):
    lax.fori_loop(0, count, lambda i, c: (body(i), c)[1], 0)


def distances(n_chip, n_col):
    return [(i, j) for i in range(n_chip) for j in range(n_col) if i + j > 0]


def step_kernel(
    sizes,
    counts, x_ref, cot_ref, w1_hbm, w2_hbm,
    bo_ref, act_hbm, grad_hbm, xk_hbm, sk_hbm, base_ref, *others,
):
    n_rep, n_row, n_col, tl, width, hidden, groups, rows, kept_rows = sizes
    near = n_rep * n_col // 2 - 1
    sent_refs, scratch = others[:near], others[near:]
    (
    w1, w2, xa, sa, scaled, xk, sk, picked, placed, back,
    part_h, part_s, came_h, came_s, result_h, result_s, packed,
    acc_h, acc_s, pair_out, pair_in, chip_out, chip_in,
    w_sem, near_send, near_recv, pair_send, pair_recv,
    part_send, part_recv, res_send, res_recv, out_sem,
    pair2_send, pair2_recv, chip_send, chip_recv,
    ) = scratch
    halves = hidden // HALF
    pack = kept_rows < rows
    unit = min(tl, MBT)
    per_block = tl // unit
    rep, row, col = (lax.axis_index(name) for name in ("rep", "row", "col"))
    core, chip = lax.rem(rep, 2), rep // 2
    n_chip = n_rep // 2
    partner = rep + 1 - 2 * core
    offsets = distances(n_chip, n_col)
    part, came = (part_h, part_s), (came_h, came_s)
    result, acc = (result_h, result_s), (acc_h, acc_s)

    def to_of(k):
        i, j = offsets[k]
        return lax.rem(chip + i, n_chip), lax.rem(col + j, n_col)

    def from_of(k):
        i, j = offsets[k]
        return lax.rem(chip + n_chip - i, n_chip), lax.rem(col + n_col - j, n_col)

    def block_to(k):
        i, j = offsets[k]
        return 1 + offsets.index(((n_chip - i) % n_chip, (n_col - j) % n_col))

    def block_rows(j, core_at):
        return rows_at((2 * j + core_at) * tl, tl)

    def size_of(i):
        return min(GROUP, hidden - i * GROUP)

    def w1_copy(i):
        return pltpu.make_async_copy(
            w1_hbm.at[:, pl.ds(i * GROUP, size_of(i))],
            w1.at[i, :, pl.ds(0, size_of(i))],
            w_sem.at[0, i],
        )

    def w2_copy(i):
        return pltpu.make_async_copy(
            w2_hbm.at[pl.ds(i * GROUP, size_of(i)), :],
            w2.at[i, pl.ds(0, size_of(i)), :],
            w_sem.at[1, i],
        )

    for i in range(groups):
        if size_of(i) < GROUP:
            w1[i, :, size_of(i):] = jnp.zeros((width, GROUP - size_of(i)), jnp.bfloat16)
            w2[i, size_of(i):, :] = jnp.zeros((GROUP - size_of(i), width), jnp.bfloat16)
        w1_copy(i).start()
    for i in range(groups):
        w2_copy(i).start()

    barrier = pltpu.get_barrier_semaphore()
    for k in range(near):
        chip_at, col_at = to_of(k)
        pl.semaphore_signal(
            barrier, inc=1, device_id=(2 * chip_at + core, row, col_at), device_id_type=MESH
        )
    pl.semaphore_signal(barrier, inc=1, device_id=(partner, row, col), device_id_type=MESH)

    @pl.when(row > 0)
    def _():
        pl.semaphore_signal(barrier, inc=1, device_id=(rep, row - 1, col), device_id_type=MESH)

    @pl.when(row < n_row - 1)
    def _():
        pl.semaphore_signal(barrier, inc=1, device_id=(rep, row + 1, col), device_id_type=MESH)

    at_ends = jnp.where(row > 0, 1, 0) + jnp.where(row < n_row - 1, 1, 0)
    pl.semaphore_wait(barrier, near + 1 + at_ends)

    def near_copy(which, source, target, k):
        chip_at, col_at = to_of(k)
        return pltpu.make_async_remote_copy(
            src_ref=source,
            dst_ref=target.at[block_rows(k + 1, core), :],
            send_sem=near_send.at[which, k],
            recv_sem=near_recv.at[which, k],
            device_id=(2 * chip_at + core, row, col_at),
            device_id_type=MESH,
        )

    def pair_copy(which, source, target, j):
        there = target.at[block_rows(j, core), :]
        return pltpu.make_async_remote_copy(
            src_ref=source if j == 0 else there,
            dst_ref=there,
            send_sem=pair_send.at[which, j],
            recv_sem=pair_recv.at[which, j],
            device_id=(partner, row, col),
            device_id_type=MESH,
        )

    def gather_start(which, source, target):
        pair_copy(which, source, target, 0).start()
        for k in range(near):
            near_copy(which, source, target, k).start()

    def gather_pass(which, source, target):
        for k in range(near):
            near_copy(which, source, target, k).wait_recv()
            pair_copy(which, source, target, k + 1).start()

    def gather_end(which, source, target):
        for j in range(1, near + 1):
            pair_copy(which, source, target, j).wait_recv()

    gather_start(0, x_ref, xa)
    xa[block_rows(0, core), :] = x_ref[...]
    counted = counts[0]
    for r in range(1, n_rep):
        counted = counted + counts[r]
    token_total = (MBT * counted).astype(jnp.float32)
    position = col * tl + lax.broadcasted_iota(jnp.int32, (tl, width), 0)
    kept = jnp.where(position < MBT * counts[rep], 1.0, 0.0)
    value = narrow(wide(cot_ref[...]) * kept / token_total)
    scaled[...] = value
    sa[block_rows(0, core), :] = value

    def place_units():
        flags = []
        for j in range(near + 1):
            chip_at, col_at = (chip, col) if j == 0 else from_of(j - 1)
            for core_at in range(2):
                for u in range(per_block):
                    batch = (col_at * tl + u * unit) // MBT
                    flags.append(jnp.where(batch < counts[2 * chip_at + core_at], 1, 0))
        total = flags[0]
        for flag in flags[1:]:
            total = total + flag
        before = 0 * total
        row_of = lax.broadcasted_iota(jnp.int32, (kept_rows, rows), 0)
        at_of = lax.broadcasted_iota(jnp.int32, (1, rows), 1)
        target = 0 * at_of
        kept_at = lax.broadcasted_iota(jnp.int32, (unit, kept_rows), 1)
        unit_at = lax.broadcasted_iota(jnp.int32, (unit, kept_rows), 0)
        for at, flag in enumerate(flags):
            first = unit * jnp.where(flag > 0, before, total + at - before)
            before = before + flag
            inside = jnp.logical_and(at_of >= at * unit, at_of < (at + 1) * unit)
            target = jnp.where(inside, first + at_of - at * unit, target)
            placed[at * unit:(at + 1) * unit, :] = narrow(
                jnp.where(kept_at == unit_at + first, 1.0, 0.0)
            )
        picked[...] = narrow(jnp.where(row_of == target, 1.0, 0.0))

    if pack:
        place_units()

    def kept_of(source, target):
        def strip(n):
            columns = rows_at(n * GROUP, GROUP)
            target[:, columns] = narrow(product(picked[...], source[:, columns]))

        each(width // GROUP, strip)

    places = (row, n_row - 1 - row)
    nexts = (row + 1, row - 1)
    furthest = jnp.maximum(row, n_row - 1 - row)
    part_runs = ((0, 0, 2 * tl), (0, 2 * tl, rows), (1, 0, kept_rows))
    result_runs = ((0, 0, rows), (1, 0, kept_rows))
    result_tick = max(len(part_runs) * groups, (n_row - 1) * LAG + 1 + groups)
    use_tick = result_tick + (n_row - 1) * LAG
    ticks = use_tick + len(result_runs) * groups

    def part_copy(run, i, d):
        kind, low, high = part_runs[run]
        return pltpu.make_async_remote_copy(
            src_ref=part[kind].at[i, d, pl.ds(low, high - low), :],
            dst_ref=came[kind].at[i, d, pl.ds(low, high - low), :],
            send_sem=part_send.at[run, i, d],
            recv_sem=part_recv.at[run, i, d],
            device_id=(rep, nexts[d], col),
            device_id_type=MESH,
        )

    def result_copy(run, i, d):
        kind, low, high = result_runs[run]
        there = result[kind].at[i, 1 - d, pl.ds(low, high - low), :]
        return pltpu.make_async_remote_copy(
            src_ref=there,
            dst_ref=there,
            send_sem=res_send.at[run, i, d],
            recv_sem=res_recv.at[run, i, d],
            device_id=(rep, nexts[d], col),
            device_id_type=MESH,
        )

    def out_copy(kind, i, h):
        source = result_s if kind == 1 else packed if pack else result_h
        target = (act_hbm, grad_hbm)[kind]
        return pltpu.make_async_copy(
            source.at[i, h],
            target.at[:, pl.ds(pl.multiple_of(i * GROUP + h * HALF, HALF), HALF)],
            out_sem.at[kind, i, h],
        )

    def make_part(run, i):
        kind, low, high = part_runs[run]
        if kind == 0:
            value = product(xa[low:high, :], w1[i])
        else:
            value = right_product(sk[...], w2[i])
        value = narrow(value)
        part[kind][i, 0, low:high, :] = value[:, :HALF]
        part[kind][i, 1, low:high, :] = value[:, HALF:]

    def finish(run, i, d):
        kind, low, high = part_runs[run]
        if kind == 0:
            total = wide(part_h[i, d, low:high, :]) + wide(came_h[i, d, low:high, :])
            result_h[i, d, low:high, :] = narrow(gelu_tanh(total))
        elif not pack:
            total = wide(part_h[i, d]) + wide(came_h[i, d])
            slope = wide(part_s[i, d]) + wide(came_s[i, d])
            result_s[i, d] = narrow(slope * gelu_slope(total))
        else:
            total = product(picked[...], part_h[i, d]) + product(picked[...], came_h[i, d])
            slope = wide(part_s[i, d]) + wide(came_s[i, d])
            result_s[i, d] = narrow(slope * gelu_slope(total))

    def add_up(kind, i):
        left = jnp.concatenate([result[kind][i, 0], result[kind][i, 1]], axis=1)

        def strip(n):
            columns = rows_at(n * GROUP, GROUP)
            if kind == 0:
                more = product(left, w2[i, :, columns])
            else:
                more = right_product(left, w1[i, columns, :])

            @pl.when(i == 0)
            def _():
                acc[kind][:, columns] = more

            @pl.when(i > 0)
            def _():
                acc[kind][:, columns] = acc[kind][:, columns] + more

        each(width // GROUP, strip)

    def tick_part(run, d, i):
        kind, low, high = part_runs[run]
        place = places[d]

        @pl.when(place > 0)
        def _():
            part_copy(run, i, d).wait_recv()

        @pl.when(jnp.logical_and(place > 0, place < n_row - 1))
        def _():
            part[kind][i, d, low:high, :] = narrow(
                wide(part[kind][i, d, low:high, :]) + wide(came[kind][i, d, low:high, :])
            )

        @pl.when(place < n_row - 1)
        def _():
            part_copy(run, i, d).start()

        @pl.when(place == n_row - 1)
        def _():
            finish(run, i, d)

    def tick_result(run, d, i):
        @pl.when(places[d] > 0)
        def _():
            result_copy(run, i, d).wait_recv()

        @pl.when(places[d] < n_row - 1)
        def _():
            result_copy(run, i, d).start()

    def acc_rows(kind, j, core_at):
        if kind == 0 or not pack:
            return acc[kind][block_rows(j, core_at), :]
        return wide(back[block_rows(j, core_at), :])

    def unpack():
        def strip(n):
            columns = rows_at(n * GROUP, GROUP)
            back[:, columns] = narrow(product(placed[...], narrow(acc_s[:, columns])))

        each(width // GROUP, strip)

    def pair2_copy(kind):
        return pltpu.make_async_remote_copy(
            src_ref=pair_out.at[kind],
            dst_ref=pair_in.at[kind],
            send_sem=pair2_send.at[kind],
            recv_sem=pair2_recv.at[kind],
            device_id=(partner, row, col),
            device_id_type=MESH,
        )

    def chip_copy(k):
        chip_at, col_at = to_of(k)
        return pltpu.make_async_remote_copy(
            src_ref=chip_out.at[k],
            dst_ref=chip_in.at[k],
            send_sem=chip_send.at[k],
            recv_sem=chip_recv.at[k],
            device_id=(2 * chip_at + core, row, col_at),
            device_id_type=MESH,
        )

    def sum_start(kind):
        for j in range(near + 1):
            pair_out[kind, j * tl:(j + 1) * tl, :] = narrow(acc_rows(kind, j, 1 - core))
        pair2_copy(kind).start()

    def both_cores(kind, j):
        return acc_rows(kind, j, core) + wide(pair_in[kind, j * tl:(j + 1) * tl, :])

    def sum_pass():
        pair2_copy(0).wait_recv()
        for k in range(near):
            chip_out[k] = narrow(both_cores(0, block_to(k)))
            chip_copy(k).start()

    def sum_end():
        total = both_cores(0, 0)
        for k in range(near):
            chip_copy(k).wait_recv()
            total = total + wide(chip_in[k])
        bo_ref[...] = narrow(wide(x_ref[...]) + total)

    def out_start(kind, i):
        for h in range(2):
            @pl.when(2 * i + h < halves)
            def _():
                out_copy(kind, i, h).start()

    def pack_result(i):
        both = jnp.concatenate([result_h[i, 0], result_h[i, 1]], axis=1)
        both = narrow(product(picked[...], both))
        packed[i, 0] = both[:, :HALF]
        packed[i, 1] = both[:, HALF:]

    x_kept, s_kept = (xk, sk) if pack else (xa, sa)
    xk_out = pltpu.make_async_copy(x_kept, xk_hbm, out_sem.at[0, groups, 0])
    sk_out = pltpu.make_async_copy(s_kept, sk_hbm, out_sem.at[0, groups, 1])
    if not pack:
        sk = sa

    for i in range(groups):
        w1_copy(i).wait()
    pair_copy(0, x_ref, xa, 0).wait_recv()
    make_part(0, 0)

    def tick(t):
        for d in range(2):
            m = t - places[d] * LAG
            for run in range(len(part_runs)):
                i = m - run * groups

                @pl.when(jnp.logical_and(i >= 0, i < groups))
                def _():
                    tick_part(run, d, i)

            for run in range(len(result_runs)):
                i = m - result_tick - run * groups

                @pl.when(jnp.logical_and(i >= 0, i < groups))
                def _():
                    tick_result(run, d, i)

        @pl.when(t == max(0, groups - 4))
        def _():
            gather_pass(0, x_ref, xa)
            gather_start(1, scaled, sa)

        @pl.when(t == groups - 1)
        def _():
            gather_end(0, x_ref, xa)

        @pl.when(t == groups)
        def _():
            if pack:
                kept_of(xa, xk)
            xk_out.start()

        @pl.when(t == groups + groups // 2)
        def _():
            gather_pass(1, scaled, sa)

        @pl.when(t == 2 * groups - 1)
        def _():
            pair_copy(1, scaled, sa, 0).wait_recv()
            gather_end(1, scaled, sa)
            if pack:
                kept_of(sa, sk)
            for i in range(groups):
                w2_copy(i).wait()
            sk_out.start()

        for run in range(len(part_runs)):
            i = t + 1 - run * groups

            @pl.when(jnp.logical_and(i >= 0, i < groups))
            def _():
                make_part(run, i)

        for kind in range(2):
            i = t - result_tick - furthest * LAG - kind * groups

            @pl.when(jnp.logical_and(i >= 0, i < groups))
            def _():
                add_up(kind, i)
                if kind == 1:
                    out_start(1, i)
                    if pack:
                        pack_result(i)
                    out_start(0, i)

        @pl.when(t == use_tick + groups)
        def _():
            sum_start(0)

        @pl.when(t == use_tick + groups + 1)
        def _():
            sum_pass()

    each(ticks, tick)
    if pack:
        unpack()
    sum_start(1)
    sum_end()
    pair2_copy(1).wait_recv()
    base_ref[...] = wide(scaled[...]) + both_cores(1, 0)
    for k in range(near):
        sent_refs[k][...] = narrow(both_cores(1, block_to(k)))

    for which, source, target in ((0, x_ref, xa), (1, scaled, sa)):
        for k in range(near):
            near_copy(which, source, target, k).wait_send()
        for j in range(near + 1):
            pair_copy(which, source, target, j).wait_send()
    for kind in range(2):
        pair2_copy(kind).wait_send()
    for k in range(near):
        chip_copy(k).wait_send()
    xk_out.wait()
    sk_out.wait()

    def drain(i):
        for d in range(2):
            @pl.when(places[d] < n_row - 1)
            def _():
                for run in range(len(part_runs)):
                    part_copy(run, i, d).wait_send()
                for run in range(len(result_runs)):
                    result_copy(run, i, d).wait_send()

            for kind in range(2):
                @pl.when(2 * i + d < halves)
                def _():
                    out_copy(kind, i, d).wait()

    each(groups, drain)


def strip_of(size, most):
    return next(strip for strip in (512, 256, 128) if strip <= most and size % strip == 0)


def weight_grads(activated, scaled, tokens, hidden_grad, block_output):
    depth, hidden = activated.shape
    width = scaled.shape[1]
    high, low = strip_of(hidden, 512), strip_of(width, 512)
    cuts = 2 if hidden % (2 * HALF) == 0 else 1
    across = hidden // cuts
    first_jobs, second_jobs = hidden // high, width // low * cuts

    def kernel(
        a_hbm, s_hbm, x_hbm, g_hbm, b_hbm, out_grad, in_grad, b_out,
        a, s, x, g, b, first_slots, second_slots, in_sem, first_sem, second_sem, b_sem,
    ):
        def a_copy(i):
            columns = rows_at(i * high, high)
            return pltpu.make_async_copy(a_hbm.at[:, columns], a.at[:, columns], in_sem.at[3 + i])

        def first_out(i):
            slot = lax.rem(i, SLOTS)
            return pltpu.make_async_copy(
                first_slots.at[slot], out_grad.at[rows_at(i * high, high), :], first_sem.at[slot]
            )

        def second_out(i):
            slot = lax.rem(i, SLOTS)
            rows, columns = rows_at(i // cuts * low, low), rows_at(lax.rem(i, cuts) * across, across)
            return pltpu.make_async_copy(
                second_slots.at[slot], in_grad.at[rows, columns], second_sem.at[slot]
            )

        s_copy = pltpu.make_async_copy(s_hbm, s, in_sem.at[0])
        x_copy = pltpu.make_async_copy(x_hbm, x, in_sem.at[1])
        g_copy = pltpu.make_async_copy(g_hbm, g, in_sem.at[2])
        b_copy = pltpu.make_async_copy(b_hbm, b, b_sem.at[0])
        b_back = pltpu.make_async_copy(b, b_out, b_sem.at[1])
        s_copy.start()
        for i in range(first_jobs):
            a_copy(i).start()
        x_copy.start()
        g_copy.start()
        b_copy.start()
        s_copy.wait()

        def first(i):
            a_copy(i).wait()

            @pl.when(i >= SLOTS)
            def _():
                first_out(i - SLOTS).wait()

            left = a[:, rows_at(i * high, high)]
            first_slots[lax.rem(i, SLOTS)] = first_product(left, s[...])
            first_out(i).start()

        each(first_jobs, first)
        x_copy.wait()
        g_copy.wait()
        b_copy.wait()
        b_back.start()

        def second(i):
            @pl.when(i >= SLOTS)
            def _():
                second_out(i - SLOTS).wait()

            left = x[:, rows_at(i // cuts * low, low)]
            right = g[:, rows_at(lax.rem(i, cuts) * across, across)]
            second_slots[lax.rem(i, SLOTS)] = first_product(left, right)
            second_out(i).start()

        each(second_jobs, second)
        for i in range(max(0, first_jobs - SLOTS), first_jobs):
            first_out(i).wait()
        for i in range(max(0, second_jobs - SLOTS), second_jobs):
            second_out(i).wait()
        b_back.wait()

    anyw = pl.BlockSpec(memory_space=pl.ANY)
    bf16, f32 = jnp.bfloat16, jnp.float32
    return pl.pallas_call(
        kernel,
        in_specs=[anyw] * 5,
        out_specs=(anyw,) * 3,
        out_shape=(
            jax.ShapeDtypeStruct((hidden, width), f32),
            jax.ShapeDtypeStruct((width, hidden), f32),
            jax.ShapeDtypeStruct(block_output.shape, bf16),
        ),
        scratch_shapes=[
            pltpu.VMEM((depth, hidden), bf16),
            pltpu.VMEM((depth, width), bf16),
            pltpu.VMEM((depth, width), bf16),
            pltpu.VMEM((depth, hidden), bf16),
            pltpu.VMEM(block_output.shape, bf16),
            pltpu.VMEM((SLOTS, high, width), f32),
            pltpu.VMEM((SLOTS, low, across), f32),
            pltpu.SemaphoreType.DMA((3 + first_jobs,)),
            pltpu.SemaphoreType.DMA((SLOTS,)),
            pltpu.SemaphoreType.DMA((SLOTS,)),
            pltpu.SemaphoreType.DMA((2,)),
        ],
        compiler_params=pltpu.CompilerParams(vmem_limit_bytes=60_000_000),
        cost_estimate=pl.CostEstimate(
            flops=4 * hidden * depth * width,
            bytes_accessed=8 * hidden * width + 4 * depth * (hidden + width),
            transcendentals=0,
        ),
    )(activated, scaled, tokens, hidden_grad, block_output)


def step(sizes, number, counts, inputs, cotangent, w_in, w_out):
    n_rep, n_row, n_col, tl, width, hidden, groups, rows, kept_rows = sizes
    blocks = n_rep * n_col // 2
    near = blocks - 1
    pack = kept_rows < rows
    spare = kept_rows if pack else 16
    bf16, f32 = jnp.bfloat16, jnp.float32
    vmem = pl.BlockSpec(memory_space=pltpu.VMEM)
    anyw = pl.BlockSpec(memory_space=pl.ANY)
    dma = pltpu.SemaphoreType.DMA
    block_output, activated, hidden_grad, tokens_kept, scaled_kept, base, *sent = pl.pallas_call(
        functools.partial(step_kernel, sizes),
        out_shape=(
            jax.ShapeDtypeStruct((tl, width), bf16),
            jax.ShapeDtypeStruct((kept_rows, hidden), bf16),
            jax.ShapeDtypeStruct((kept_rows, hidden), bf16),
            jax.ShapeDtypeStruct((kept_rows, width), bf16),
            jax.ShapeDtypeStruct((kept_rows, width), bf16),
            jax.ShapeDtypeStruct((tl, width), f32),
            *[jax.ShapeDtypeStruct((tl, width), bf16)] * near,
        ),
        in_specs=[pl.BlockSpec(memory_space=pltpu.SMEM), vmem, vmem, anyw, anyw],
        out_specs=(vmem, anyw, anyw, anyw, anyw, vmem, *[vmem] * near),
        scratch_shapes=[
            pltpu.VMEM((groups, width, GROUP), bf16),
            pltpu.VMEM((groups, GROUP, width), bf16),
            pltpu.VMEM((rows, width), bf16),
            pltpu.VMEM((rows, width), bf16),
            pltpu.VMEM((tl, width), bf16),
            pltpu.VMEM((spare, width), bf16),
            pltpu.VMEM((spare, width), bf16),
            pltpu.VMEM((spare, rows), bf16),
            pltpu.VMEM((rows, spare), bf16),
            pltpu.VMEM((rows if pack else 16, width), bf16),
            pltpu.VMEM((groups, 2, rows, HALF), bf16),
            pltpu.VMEM((groups, 2, kept_rows, HALF), bf16),
            pltpu.VMEM((groups, 2, rows, HALF), bf16),
            pltpu.VMEM((groups, 2, kept_rows, HALF), bf16),
            pltpu.VMEM((groups, 2, rows, HALF), bf16),
            pltpu.VMEM((groups, 2, kept_rows, HALF), bf16),
            pltpu.VMEM((groups, 2, spare, HALF), bf16),
            pltpu.VMEM((rows, width), f32),
            pltpu.VMEM((kept_rows, width), f32),
            pltpu.VMEM((2, blocks * tl, width), bf16),
            pltpu.VMEM((2, blocks * tl, width), bf16),
            pltpu.VMEM((near, tl, width), bf16),
            pltpu.VMEM((near, tl, width), bf16),
            dma((2, groups)),
            dma((2, near)),
            dma((2, near)),
            dma((2, near + 1)),
            dma((2, near + 1)),
            dma((3, groups, 2)),
            dma((3, groups, 2)),
            dma((2, groups, 2)),
            dma((2, groups, 2)),
            dma((2, groups + 1, 2)),
            dma((2,)),
            dma((2,)),
            dma((near,)),
            dma((near,)),
        ],
        compiler_params=pltpu.CompilerParams(
            collective_id=number, has_side_effects=True, vmem_limit_bytes=67_000_000
        ),
    )(counts, inputs, cotangent, w_in, w_out)
    n_chip = n_rep // 2
    total = base
    for (i, j), own in zip(distances(n_chip, n_col), sent):
        pairs = [
            (
                (2 * chip + core) * n_col + col,
                (2 * ((chip + i) % n_chip) + core) * n_col + (col + j) % n_col,
            )
            for chip in range(n_chip) for core in range(2) for col in range(n_col)
        ]
        total = total + wide(lax.ppermute(own, ("rep", "col"), pairs))
    w_out_grad, w_in_grad, block_output = weight_grads(
        activated, scaled_kept, tokens_kept, hidden_grad, block_output
    )
    return block_output, narrow(total), w_in_grad, w_out_grad


def body(inputs, w_in, w_out, cotangent, counts):
    tl, width = inputs.shape[1], inputs.shape[2]
    hidden = w_in.shape[1]
    n_rep, n_row, n_col = (lax.axis_size(name) for name in ("rep", "row", "col"))
    rows = n_rep * n_col * tl
    cases = [rows * eighths // 8 for eighths in EIGHTHS]
    sizes = (n_rep, n_row, n_col, tl, width, hidden, -(-hidden // GROUP), rows)
    kept_rows = MBT * jnp.sum(counts)
    case = sum((kept_rows > rows_of_case).astype(jnp.int32) for rows_of_case in cases[:-1])
    args = (
        counts, inputs.reshape(tl, width), cotangent.reshape(tl, width), w_in, w_out
    )
    branches = [
        functools.partial(step, (*sizes, kept), number) for number, kept in enumerate(cases)
    ]
    if len(branches) == 1:
        block_output, input_grad, w_in_grad, w_out_grad = branches[0](*args)
    else:
        block_output, input_grad, w_in_grad, w_out_grad = lax.switch(case, branches, *args)
    return (
        block_output.reshape(1, tl, width),
        input_grad.reshape(1, tl, width),
        w_in_grad,
        w_out_grad,
    )


def solution(mesh):
    placed = (
        P("rep", "col", "row"),
        P("row", ("rep", "col")),
        P(("rep", "col"), "row"),
        P("rep", "col", "row"),
        P(),
    )
    return jax.shard_map(
        body,
        mesh=mesh,
        in_specs=placed,
        out_specs=(
            P("rep", "col", "row"),
            P("rep", "col", "row"),
            P("row", ("rep", "col")),
            P(("rep", "col"), "row"),
        ),
        check_vma=False,
    )
```

```python
import functools

import jax
import jax.numpy as jnp
from jax import lax
from jax.experimental import pallas as pl
from jax.experimental.pallas import tpu as pltpu
from jax.sharding import PartitionSpec as P

MBT = 32
HALF = 128
GROUP = 2 * HALF
LAG = 3
SLOTS = 3
EIGHTHS = (4, 5, 6, 8)
MESH = pl.DeviceIdType.MESH

root_coef = 0.7978845608028654
cubic_coef = 0.044715


def gelu_tanh(values):
    inner = root_coef * (values + cubic_coef * values * values * values)
    return 0.5 * values * (1.0 + jnp.tanh(inner))


def gelu_slope(values):
    inner = root_coef * (values + cubic_coef * values * values * values)
    tangent = jnp.tanh(inner)
    return 0.5 * (1.0 + tangent) + 0.5 * values * (1.0 - tangent * tangent) * root_coef * (
        1.0 + 3.0 * cubic_coef * values * values
    )


def wide(values):
    return values.astype(jnp.float32)


def narrow(values):
    return values.astype(jnp.bfloat16)


def product(left, right):
    return jnp.dot(left, right, preferred_element_type=jnp.float32)


def right_product(left, right):
    return lax.dot_general(
        left, right, (((1,), (1,)), ((), ())), preferred_element_type=jnp.float32
    )


def first_product(left, right):
    return lax.dot_general(
        left, right, (((0,), (0,)), ((), ())), preferred_element_type=jnp.float32
    )


def rows_at(start, size):
    return pl.ds(pl.multiple_of(start, size), size)


def each(count, body):
    lax.fori_loop(0, count, lambda i, c: (body(i), c)[1], 0)


def distances(n_chip, n_col):
    return [(i, j) for i in range(n_chip) for j in range(n_col) if i + j > 0]


def step_kernel(
    sizes,
    counts, x_ref, cot_ref, w1_hbm, w2_hbm,
    bo_ref, act_hbm, grad_hbm, xk_hbm, sk_hbm, base_ref, *others,
):
    n_rep, n_row, n_col, tl, width, hidden, groups, rows, kept_rows = sizes
    near = n_rep * n_col // 2 - 1
    sent_refs, scratch = others[:near], others[near:]
    (
    w1, w2, xa, sa, scaled, xk, sk, picked, placed, back,
    part_h, part_s, came_h, came_s, result_h, result_s, packed,
    acc_h, acc_s, pair_out, pair_in, chip_out, chip_in,
    w_sem, near_send, near_recv, pair_send, pair_recv,
    part_send, part_recv, res_send, res_recv, out_sem,
    pair2_send, pair2_recv, chip_send, chip_recv,
    ) = scratch
    halves = hidden // HALF
    pack = kept_rows < rows
    unit = min(tl, MBT)
    per_block = tl // unit
    rep, row, col = (lax.axis_index(name) for name in ("rep", "row", "col"))
    core, chip = lax.rem(rep, 2), rep // 2
    n_chip = n_rep // 2
    partner = rep + 1 - 2 * core
    offsets = distances(n_chip, n_col)
    part, came = (part_h, part_s), (came_h, came_s)
    result, acc = (result_h, result_s), (acc_h, acc_s)

    def to_of(k):
        i, j = offsets[k]
        return lax.rem(chip + i, n_chip), lax.rem(col + j, n_col)

    def from_of(k):
        i, j = offsets[k]
        return lax.rem(chip + n_chip - i, n_chip), lax.rem(col + n_col - j, n_col)

    def block_to(k):
        i, j = offsets[k]
        return 1 + offsets.index(((n_chip - i) % n_chip, (n_col - j) % n_col))

    def block_rows(j, core_at):
        return rows_at((2 * j + core_at) * tl, tl)

    def size_of(i):
        return min(GROUP, hidden - i * GROUP)

    def w1_copy(i):
        return pltpu.make_async_copy(
            w1_hbm.at[:, pl.ds(i * GROUP, size_of(i))],
            w1.at[i, :, pl.ds(0, size_of(i))],
            w_sem.at[0, i],
        )

    def w2_copy(i):
        return pltpu.make_async_copy(
            w2_hbm.at[pl.ds(i * GROUP, size_of(i)), :],
            w2.at[i, pl.ds(0, size_of(i)), :],
            w_sem.at[1, i],
        )

    for i in range(groups):
        if size_of(i) < GROUP:
            w1[i, :, size_of(i):] = jnp.zeros((width, GROUP - size_of(i)), jnp.bfloat16)
            w2[i, size_of(i):, :] = jnp.zeros((GROUP - size_of(i), width), jnp.bfloat16)
        w1_copy(i).start()
    for i in range(groups):
        w2_copy(i).start()

    barrier = pltpu.get_barrier_semaphore()
    for k in range(near):
        chip_at, col_at = to_of(k)
        pl.semaphore_signal(
            barrier, inc=1, device_id=(2 * chip_at + core, row, col_at), device_id_type=MESH
        )
    pl.semaphore_signal(barrier, inc=1, device_id=(partner, row, col), device_id_type=MESH)

    @pl.when(row > 0)
    def _():
        pl.semaphore_signal(barrier, inc=1, device_id=(rep, row - 1, col), device_id_type=MESH)

    @pl.when(row < n_row - 1)
    def _():
        pl.semaphore_signal(barrier, inc=1, device_id=(rep, row + 1, col), device_id_type=MESH)

    at_ends = jnp.where(row > 0, 1, 0) + jnp.where(row < n_row - 1, 1, 0)
    pl.semaphore_wait(barrier, near + 1 + at_ends)

    def near_copy(which, source, target, k):
        chip_at, col_at = to_of(k)
        return pltpu.make_async_remote_copy(
            src_ref=source,
            dst_ref=target.at[block_rows(k + 1, core), :],
            send_sem=near_send.at[which, k],
            recv_sem=near_recv.at[which, k],
            device_id=(2 * chip_at + core, row, col_at),
            device_id_type=MESH,
        )

    def pair_copy(which, source, target, j):
        there = target.at[block_rows(j, core), :]
        return pltpu.make_async_remote_copy(
            src_ref=source if j == 0 else there,
            dst_ref=there,
            send_sem=pair_send.at[which, j],
            recv_sem=pair_recv.at[which, j],
            device_id=(partner, row, col),
            device_id_type=MESH,
        )

    def gather_start(which, source, target):
        pair_copy(which, source, target, 0).start()
        for k in range(near):
            near_copy(which, source, target, k).start()

    def gather_pass(which, source, target):
        for k in range(near):
            near_copy(which, source, target, k).wait_recv()
            pair_copy(which, source, target, k + 1).start()

    def gather_end(which, source, target):
        for j in range(1, near + 1):
            pair_copy(which, source, target, j).wait_recv()

    gather_start(0, x_ref, xa)
    xa[block_rows(0, core), :] = x_ref[...]
    counted = counts[0]
    for r in range(1, n_rep):
        counted = counted + counts[r]
    token_total = (MBT * counted).astype(jnp.float32)
    position = col * tl + lax.broadcasted_iota(jnp.int32, (tl, width), 0)
    kept = jnp.where(position < MBT * counts[rep], 1.0, 0.0)
    value = narrow(wide(cot_ref[...]) * kept / token_total)
    scaled[...] = value
    sa[block_rows(0, core), :] = value

    def place_units():
        flags = []
        for j in range(near + 1):
            chip_at, col_at = (chip, col) if j == 0 else from_of(j - 1)
            for core_at in range(2):
                for u in range(per_block):
                    batch = (col_at * tl + u * unit) // MBT
                    flags.append(jnp.where(batch < counts[2 * chip_at + core_at], 1, 0))
        total = flags[0]
        for flag in flags[1:]:
            total = total + flag
        before = 0 * total
        row_of = lax.broadcasted_iota(jnp.int32, (kept_rows, rows), 0)
        at_of = lax.broadcasted_iota(jnp.int32, (1, rows), 1)
        target = 0 * at_of
        kept_at = lax.broadcasted_iota(jnp.int32, (unit, kept_rows), 1)
        unit_at = lax.broadcasted_iota(jnp.int32, (unit, kept_rows), 0)
        for at, flag in enumerate(flags):
            first = unit * jnp.where(flag > 0, before, total + at - before)
            before = before + flag
            inside = jnp.logical_and(at_of >= at * unit, at_of < (at + 1) * unit)
            target = jnp.where(inside, first + at_of - at * unit, target)
            placed[at * unit:(at + 1) * unit, :] = narrow(
                jnp.where(kept_at == unit_at + first, 1.0, 0.0)
            )
        picked[...] = narrow(jnp.where(row_of == target, 1.0, 0.0))

    if pack:
        place_units()

    def kept_of(source, target):
        target[...] = narrow(product(picked[...], source[...]))

    places = (row, n_row - 1 - row)
    nexts = (row + 1, row - 1)
    furthest = jnp.maximum(row, n_row - 1 - row)
    part_runs = ((0, 0, 2 * tl), (0, 2 * tl, rows), (1, 0, kept_rows))
    result_runs = ((0, 0, rows), (1, 0, kept_rows))
    result_tick = max(len(part_runs) * groups, (n_row - 1) * LAG + 1 + groups)
    use_tick = result_tick + (n_row - 1) * LAG
    ticks = use_tick + len(result_runs) * groups

    def part_copy(run, i, d):
        kind, low, high = part_runs[run]
        return pltpu.make_async_remote_copy(
            src_ref=part[kind].at[i, d, pl.ds(low, high - low), :],
            dst_ref=came[kind].at[i, d, pl.ds(low, high - low), :],
            send_sem=part_send.at[run, i, d],
            recv_sem=part_recv.at[run, i, d],
            device_id=(rep, nexts[d], col),
            device_id_type=MESH,
        )

    def result_copy(run, i, d):
        kind, low, high = result_runs[run]
        there = result[kind].at[i, 1 - d, pl.ds(low, high - low), :]
        return pltpu.make_async_remote_copy(
            src_ref=there,
            dst_ref=there,
            send_sem=res_send.at[run, i, d],
            recv_sem=res_recv.at[run, i, d],
            device_id=(rep, nexts[d], col),
            device_id_type=MESH,
        )

    def out_copy(kind, i, h):
        source = result_s if kind == 1 else packed if pack else result_h
        target = (act_hbm, grad_hbm)[kind]
        return pltpu.make_async_copy(
            source.at[i, h],
            target.at[:, pl.ds(pl.multiple_of(i * GROUP + h * HALF, HALF), HALF)],
            out_sem.at[kind, i, h],
        )

    def make_part(run, i):
        kind, low, high = part_runs[run]
        if kind == 0:
            value = product(xa[low:high, :], w1[i])
        else:
            value = right_product(sk[...], w2[i])
        value = narrow(value)
        part[kind][i, 0, low:high, :] = value[:, :HALF]
        part[kind][i, 1, low:high, :] = value[:, HALF:]

    def finish(run, i, d):
        kind, low, high = part_runs[run]
        if kind == 0:
            total = wide(part_h[i, d, low:high, :]) + wide(came_h[i, d, low:high, :])
            result_h[i, d, low:high, :] = narrow(gelu_tanh(total))
        elif not pack:
            total = wide(part_h[i, d]) + wide(came_h[i, d])
            slope = wide(part_s[i, d]) + wide(came_s[i, d])
            result_s[i, d] = narrow(slope * gelu_slope(total))
        else:
            total = product(picked[...], part_h[i, d]) + product(picked[...], came_h[i, d])
            slope = wide(part_s[i, d]) + wide(came_s[i, d])
            result_s[i, d] = narrow(slope * gelu_slope(total))

    def add_up(kind, i):
        left = jnp.concatenate([result[kind][i, 0], result[kind][i, 1]], axis=1)
        more = product(left, w2[i]) if kind == 0 else right_product(left, w1[i])

        @pl.when(i == 0)
        def _():
            acc[kind][...] = more

        @pl.when(i > 0)
        def _():
            acc[kind][...] = acc[kind][...] + more

    def tick_part(run, d, i):
        kind, low, high = part_runs[run]
        place = places[d]

        @pl.when(place > 0)
        def _():
            part_copy(run, i, d).wait_recv()

        @pl.when(jnp.logical_and(place > 0, place < n_row - 1))
        def _():
            part[kind][i, d, low:high, :] = narrow(
                wide(part[kind][i, d, low:high, :]) + wide(came[kind][i, d, low:high, :])
            )

        @pl.when(place < n_row - 1)
        def _():
            part_copy(run, i, d).start()

        @pl.when(place == n_row - 1)
        def _():
            finish(run, i, d)

    def tick_result(run, d, i):
        @pl.when(places[d] > 0)
        def _():
            result_copy(run, i, d).wait_recv()

        @pl.when(places[d] < n_row - 1)
        def _():
            result_copy(run, i, d).start()

    def acc_rows(kind, j, core_at):
        if kind == 0 or not pack:
            return acc[kind][block_rows(j, core_at), :]
        return wide(back[block_rows(j, core_at), :])

    def unpack():
        back[...] = narrow(product(placed[...], narrow(acc_s[...])))

    def pair2_copy(kind):
        return pltpu.make_async_remote_copy(
            src_ref=pair_out.at[kind],
            dst_ref=pair_in.at[kind],
            send_sem=pair2_send.at[kind],
            recv_sem=pair2_recv.at[kind],
            device_id=(partner, row, col),
            device_id_type=MESH,
        )

    def chip_copy(k):
        chip_at, col_at = to_of(k)
        return pltpu.make_async_remote_copy(
            src_ref=chip_out.at[k],
            dst_ref=chip_in.at[k],
            send_sem=chip_send.at[k],
            recv_sem=chip_recv.at[k],
            device_id=(2 * chip_at + core, row, col_at),
            device_id_type=MESH,
        )

    def sum_start(kind):
        for j in range(near + 1):
            pair_out[kind, j * tl:(j + 1) * tl, :] = narrow(acc_rows(kind, j, 1 - core))
        pair2_copy(kind).start()

    def both_cores(kind, j):
        return acc_rows(kind, j, core) + wide(pair_in[kind, j * tl:(j + 1) * tl, :])

    def sum_pass():
        pair2_copy(0).wait_recv()
        for k in range(near):
            chip_out[k] = narrow(both_cores(0, block_to(k)))
            chip_copy(k).start()

    def sum_end():
        total = both_cores(0, 0)
        for k in range(near):
            chip_copy(k).wait_recv()
            total = total + wide(chip_in[k])
        bo_ref[...] = narrow(wide(x_ref[...]) + total)

    def out_start(kind, i):
        for h in range(2):
            @pl.when(2 * i + h < halves)
            def _():
                out_copy(kind, i, h).start()

    def pack_result(i):
        both = jnp.concatenate([result_h[i, 0], result_h[i, 1]], axis=1)
        both = narrow(product(picked[...], both))
        packed[i, 0] = both[:, :HALF]
        packed[i, 1] = both[:, HALF:]

    x_kept, s_kept = (xk, sk) if pack else (xa, sa)
    xk_out = pltpu.make_async_copy(x_kept, xk_hbm, out_sem.at[0, groups, 0])
    sk_out = pltpu.make_async_copy(s_kept, sk_hbm, out_sem.at[0, groups, 1])
    if not pack:
        sk = sa

    for i in range(groups):
        w1_copy(i).wait()
    pair_copy(0, x_ref, xa, 0).wait_recv()
    make_part(0, 0)

    def tick(t):
        for d in range(2):
            m = t - places[d] * LAG
            for run in range(len(part_runs)):
                i = m - run * groups

                @pl.when(jnp.logical_and(i >= 0, i < groups))
                def _():
                    tick_part(run, d, i)

            for run in range(len(result_runs)):
                i = m - result_tick - run * groups

                @pl.when(jnp.logical_and(i >= 0, i < groups))
                def _():
                    tick_result(run, d, i)

        @pl.when(t == max(0, groups - 4))
        def _():
            gather_pass(0, x_ref, xa)
            gather_start(1, scaled, sa)

        @pl.when(t == groups - 1)
        def _():
            gather_end(0, x_ref, xa)

        @pl.when(t == groups)
        def _():
            if pack:
                kept_of(xa, xk)
            xk_out.start()

        @pl.when(t == groups + groups // 2)
        def _():
            gather_pass(1, scaled, sa)

        @pl.when(t == 2 * groups - 1)
        def _():
            pair_copy(1, scaled, sa, 0).wait_recv()
            gather_end(1, scaled, sa)
            if pack:
                kept_of(sa, sk)
            for i in range(groups):
                w2_copy(i).wait()
            sk_out.start()

        for run in range(len(part_runs)):
            i = t + 1 - run * groups

            @pl.when(jnp.logical_and(i >= 0, i < groups))
            def _():
                make_part(run, i)

        for kind in range(2):
            i = t - result_tick - furthest * LAG - kind * groups

            @pl.when(jnp.logical_and(i >= 0, i < groups))
            def _():
                add_up(kind, i)
                if kind == 1:
                    out_start(1, i)
                    if pack:
                        pack_result(i)
                    out_start(0, i)

        @pl.when(t == use_tick + groups)
        def _():
            sum_start(0)

        @pl.when(t == use_tick + groups + 1)
        def _():
            sum_pass()

    each(ticks, tick)
    if pack:
        unpack()
    sum_start(1)
    sum_end()
    pair2_copy(1).wait_recv()
    base_ref[...] = wide(scaled[...]) + both_cores(1, 0)
    for k in range(near):
        sent_refs[k][...] = narrow(both_cores(1, block_to(k)))

    for which, source, target in ((0, x_ref, xa), (1, scaled, sa)):
        for k in range(near):
            near_copy(which, source, target, k).wait_send()
        for j in range(near + 1):
            pair_copy(which, source, target, j).wait_send()
    for kind in range(2):
        pair2_copy(kind).wait_send()
    for k in range(near):
        chip_copy(k).wait_send()
    xk_out.wait()
    sk_out.wait()

    def drain(i):
        for d in range(2):
            @pl.when(places[d] < n_row - 1)
            def _():
                for run in range(len(part_runs)):
                    part_copy(run, i, d).wait_send()
                for run in range(len(result_runs)):
                    result_copy(run, i, d).wait_send()

            for kind in range(2):
                @pl.when(2 * i + d < halves)
                def _():
                    out_copy(kind, i, d).wait()

    each(groups, drain)


def strip_of(size, most):
    return next(strip for strip in (512, 256, 128) if strip <= most and size % strip == 0)


def weight_grads(activated, scaled, tokens, hidden_grad, block_output):
    depth, hidden = activated.shape
    width = scaled.shape[1]
    high, low = strip_of(hidden, 512), strip_of(width, 512)
    cuts = 2 if hidden % (2 * HALF) == 0 else 1
    across = hidden // cuts
    first_jobs, second_jobs = hidden // high, width // low * cuts

    def kernel(
        a_hbm, s_hbm, x_hbm, g_hbm, b_hbm, out_grad, in_grad, b_out,
        a, s, x, g, b, first_slots, second_slots, in_sem, first_sem, second_sem, b_sem,
    ):
        def a_copy(i):
            columns = rows_at(i * high, high)
            return pltpu.make_async_copy(a_hbm.at[:, columns], a.at[:, columns], in_sem.at[3 + i])

        def first_out(i):
            slot = lax.rem(i, SLOTS)
            return pltpu.make_async_copy(
                first_slots.at[slot], out_grad.at[rows_at(i * high, high), :], first_sem.at[slot]
            )

        def second_out(i):
            slot = lax.rem(i, SLOTS)
            rows, columns = rows_at(i // cuts * low, low), rows_at(lax.rem(i, cuts) * across, across)
            return pltpu.make_async_copy(
                second_slots.at[slot], in_grad.at[rows, columns], second_sem.at[slot]
            )

        s_copy = pltpu.make_async_copy(s_hbm, s, in_sem.at[0])
        x_copy = pltpu.make_async_copy(x_hbm, x, in_sem.at[1])
        g_copy = pltpu.make_async_copy(g_hbm, g, in_sem.at[2])
        b_copy = pltpu.make_async_copy(b_hbm, b, b_sem.at[0])
        b_back = pltpu.make_async_copy(b, b_out, b_sem.at[1])
        s_copy.start()
        for i in range(first_jobs):
            a_copy(i).start()
        x_copy.start()
        g_copy.start()
        b_copy.start()
        s_copy.wait()

        def first(i):
            a_copy(i).wait()

            @pl.when(i >= SLOTS)
            def _():
                first_out(i - SLOTS).wait()

            left = a[:, rows_at(i * high, high)]
            first_slots[lax.rem(i, SLOTS)] = first_product(left, s[...])
            first_out(i).start()

        each(first_jobs, first)
        x_copy.wait()
        g_copy.wait()
        b_copy.wait()
        b_back.start()

        def second(i):
            @pl.when(i >= SLOTS)
            def _():
                second_out(i - SLOTS).wait()

            left = x[:, rows_at(i // cuts * low, low)]
            right = g[:, rows_at(lax.rem(i, cuts) * across, across)]
            second_slots[lax.rem(i, SLOTS)] = first_product(left, right)
            second_out(i).start()

        each(second_jobs, second)
        for i in range(max(0, first_jobs - SLOTS), first_jobs):
            first_out(i).wait()
        for i in range(max(0, second_jobs - SLOTS), second_jobs):
            second_out(i).wait()
        b_back.wait()

    anyw = pl.BlockSpec(memory_space=pl.ANY)
    bf16, f32 = jnp.bfloat16, jnp.float32
    return pl.pallas_call(
        kernel,
        in_specs=[anyw] * 5,
        out_specs=(anyw,) * 3,
        out_shape=(
            jax.ShapeDtypeStruct((hidden, width), f32),
            jax.ShapeDtypeStruct((width, hidden), f32),
            jax.ShapeDtypeStruct(block_output.shape, bf16),
        ),
        scratch_shapes=[
            pltpu.VMEM((depth, hidden), bf16),
            pltpu.VMEM((depth, width), bf16),
            pltpu.VMEM((depth, width), bf16),
            pltpu.VMEM((depth, hidden), bf16),
            pltpu.VMEM(block_output.shape, bf16),
            pltpu.VMEM((SLOTS, high, width), f32),
            pltpu.VMEM((SLOTS, low, across), f32),
            pltpu.SemaphoreType.DMA((3 + first_jobs,)),
            pltpu.SemaphoreType.DMA((SLOTS,)),
            pltpu.SemaphoreType.DMA((SLOTS,)),
            pltpu.SemaphoreType.DMA((2,)),
        ],
        compiler_params=pltpu.CompilerParams(vmem_limit_bytes=60_000_000),
        cost_estimate=pl.CostEstimate(
            flops=4 * hidden * depth * width,
            bytes_accessed=8 * hidden * width + 4 * depth * (hidden + width),
            transcendentals=0,
        ),
    )(activated, scaled, tokens, hidden_grad, block_output)


def step(sizes, number, counts, inputs, cotangent, w_in, w_out):
    n_rep, n_row, n_col, tl, width, hidden, groups, rows, kept_rows = sizes
    blocks = n_rep * n_col // 2
    near = blocks - 1
    pack = kept_rows < rows
    spare = kept_rows if pack else 16
    bf16, f32 = jnp.bfloat16, jnp.float32
    vmem = pl.BlockSpec(memory_space=pltpu.VMEM)
    anyw = pl.BlockSpec(memory_space=pl.ANY)
    dma = pltpu.SemaphoreType.DMA
    block_output, activated, hidden_grad, tokens_kept, scaled_kept, base, *sent = pl.pallas_call(
        functools.partial(step_kernel, sizes),
        out_shape=(
            jax.ShapeDtypeStruct((tl, width), bf16),
            jax.ShapeDtypeStruct((kept_rows, hidden), bf16),
            jax.ShapeDtypeStruct((kept_rows, hidden), bf16),
            jax.ShapeDtypeStruct((kept_rows, width), bf16),
            jax.ShapeDtypeStruct((kept_rows, width), bf16),
            jax.ShapeDtypeStruct((tl, width), f32),
            *[jax.ShapeDtypeStruct((tl, width), bf16)] * near,
        ),
        in_specs=[pl.BlockSpec(memory_space=pltpu.SMEM), vmem, vmem, anyw, anyw],
        out_specs=(vmem, anyw, anyw, anyw, anyw, vmem, *[vmem] * near),
        scratch_shapes=[
            pltpu.VMEM((groups, width, GROUP), bf16),
            pltpu.VMEM((groups, GROUP, width), bf16),
            pltpu.VMEM((rows, width), bf16),
            pltpu.VMEM((rows, width), bf16),
            pltpu.VMEM((tl, width), bf16),
            pltpu.VMEM((spare, width), bf16),
            pltpu.VMEM((spare, width), bf16),
            pltpu.VMEM((spare, rows), bf16),
            pltpu.VMEM((rows, spare), bf16),
            pltpu.VMEM((rows if pack else 16, width), bf16),
            pltpu.VMEM((groups, 2, rows, HALF), bf16),
            pltpu.VMEM((groups, 2, kept_rows, HALF), bf16),
            pltpu.VMEM((groups, 2, rows, HALF), bf16),
            pltpu.VMEM((groups, 2, kept_rows, HALF), bf16),
            pltpu.VMEM((groups, 2, rows, HALF), bf16),
            pltpu.VMEM((groups, 2, kept_rows, HALF), bf16),
            pltpu.VMEM((groups, 2, spare, HALF), bf16),
            pltpu.VMEM((rows, width), f32),
            pltpu.VMEM((kept_rows, width), f32),
            pltpu.VMEM((2, blocks * tl, width), bf16),
            pltpu.VMEM((2, blocks * tl, width), bf16),
            pltpu.VMEM((near, tl, width), bf16),
            pltpu.VMEM((near, tl, width), bf16),
            dma((2, groups)),
            dma((2, near)),
            dma((2, near)),
            dma((2, near + 1)),
            dma((2, near + 1)),
            dma((3, groups, 2)),
            dma((3, groups, 2)),
            dma((2, groups, 2)),
            dma((2, groups, 2)),
            dma((2, groups + 1, 2)),
            dma((2,)),
            dma((2,)),
            dma((near,)),
            dma((near,)),
        ],
        compiler_params=pltpu.CompilerParams(
            collective_id=number, has_side_effects=True, vmem_limit_bytes=67_000_000
        ),
    )(counts, inputs, cotangent, w_in, w_out)
    n_chip = n_rep // 2
    total = base
    for (i, j), own in zip(distances(n_chip, n_col), sent):
        pairs = [
            (
                (2 * chip + core) * n_col + col,
                (2 * ((chip + i) % n_chip) + core) * n_col + (col + j) % n_col,
            )
            for chip in range(n_chip) for core in range(2) for col in range(n_col)
        ]
        total = total + wide(lax.ppermute(own, ("rep", "col"), pairs))
    w_out_grad, w_in_grad, block_output = weight_grads(
        activated, scaled_kept, tokens_kept, hidden_grad, block_output
    )
    return block_output, narrow(total), w_in_grad, w_out_grad


def body(inputs, w_in, w_out, cotangent, counts):
    tl, width = inputs.shape[1], inputs.shape[2]
    hidden = w_in.shape[1]
    n_rep, n_row, n_col = (lax.axis_size(name) for name in ("rep", "row", "col"))
    rows = n_rep * n_col * tl
    cases = [rows * eighths // 8 for eighths in EIGHTHS]
    sizes = (n_rep, n_row, n_col, tl, width, hidden, -(-hidden // GROUP), rows)
    kept_rows = MBT * jnp.sum(counts)
    case = sum((kept_rows > rows_of_case).astype(jnp.int32) for rows_of_case in cases[:-1])
    args = (
        counts, inputs.reshape(tl, width), cotangent.reshape(tl, width), w_in, w_out
    )
    branches = [
        functools.partial(step, (*sizes, kept), number) for number, kept in enumerate(cases)
    ]
    if len(branches) == 1:
        block_output, input_grad, w_in_grad, w_out_grad = branches[0](*args)
    else:
        block_output, input_grad, w_in_grad, w_out_grad = lax.switch(case, branches, *args)
    return (
        block_output.reshape(1, tl, width),
        input_grad.reshape(1, tl, width),
        w_in_grad,
        w_out_grad,
    )


def solution(mesh):
    placed = (
        P("rep", "col", "row"),
        P("row", ("rep", "col")),
        P(("rep", "col"), "row"),
        P("rep", "col", "row"),
        P(),
    )
    return jax.shard_map(
        body,
        mesh=mesh,
        in_specs=placed,
        out_specs=(
            P("rep", "col", "row"),
            P("rep", "col", "row"),
            P("row", ("rep", "col")),
            P(("rep", "col"), "row"),
        ),
        check_vma=False,
    )
```

```python
import functools

import jax
import jax.numpy as jnp
from jax import lax
from jax.experimental import pallas as pl
from jax.experimental.pallas import tpu as pltpu
from jax.sharding import PartitionSpec as P

MBT = 32
HALF = 128
GROUP = 2 * HALF
LAG = 3
SLOTS = 3
EIGHTHS = (4, 5, 6, 8)
MESH = pl.DeviceIdType.MESH

root_coef = 0.7978845608028654
cubic_coef = 0.044715


def gelu_tanh(values):
    inner = root_coef * (values + cubic_coef * values * values * values)
    return 0.5 * values * (1.0 + jnp.tanh(inner))


def gelu_slope(values):
    inner = root_coef * (values + cubic_coef * values * values * values)
    tangent = jnp.tanh(inner)
    return 0.5 * (1.0 + tangent) + 0.5 * values * (1.0 - tangent * tangent) * root_coef * (
        1.0 + 3.0 * cubic_coef * values * values
    )


def wide(values):
    return values.astype(jnp.float32)


def narrow(values):
    return values.astype(jnp.bfloat16)


def product(left, right):
    return jnp.dot(left, right, preferred_element_type=jnp.float32)


def right_product(left, right):
    return lax.dot_general(
        left, right, (((1,), (1,)), ((), ())), preferred_element_type=jnp.float32
    )


def first_product(left, right):
    return lax.dot_general(
        left, right, (((0,), (0,)), ((), ())), preferred_element_type=jnp.float32
    )


def rows_at(start, size):
    return pl.ds(pl.multiple_of(start, size), size)


def each(count, body):
    lax.fori_loop(0, count, lambda i, c: (body(i), c)[1], 0)


def distances(n_chip, n_col):
    return [(i, j) for i in range(n_chip) for j in range(n_col) if i + j > 0]


def step_kernel(
    sizes,
    counts, x_ref, cot_ref, w1_hbm, w2_hbm,
    bo_ref, act_hbm, grad_hbm, xk_hbm, sk_hbm, base_ref, *others,
):
    n_rep, n_row, n_col, tl, width, hidden, groups, rows, kept_rows = sizes
    near = n_rep * n_col // 2 - 1
    sent_refs, scratch = others[:near], others[near:]
    (
    w1, w2, xa, sa, scaled, xk, sk, picked, placed, back,
    part_h, part_s, came_h, came_s, result_h, result_s, packed,
    acc_h, acc_s, pair_out, pair_in, chip_out, chip_in,
    w_sem, near_send, near_recv, pair_send, pair_recv,
    part_send, part_recv, res_send, res_recv, out_sem,
    pair2_send, pair2_recv, chip_send, chip_recv,
    ) = scratch
    halves = hidden // HALF
    pack = kept_rows < rows
    unit = min(tl, MBT)
    per_block = tl // unit
    rep, row, col = (lax.axis_index(name) for name in ("rep", "row", "col"))
    core, chip = lax.rem(rep, 2), rep // 2
    n_chip = n_rep // 2
    partner = rep + 1 - 2 * core
    offsets = distances(n_chip, n_col)
    part, came = (part_h, part_s), (came_h, came_s)
    result, acc = (result_h, result_s), (acc_h, acc_s)

    def to_of(k):
        i, j = offsets[k]
        return lax.rem(chip + i, n_chip), lax.rem(col + j, n_col)

    def from_of(k):
        i, j = offsets[k]
        return lax.rem(chip + n_chip - i, n_chip), lax.rem(col + n_col - j, n_col)

    def block_to(k):
        i, j = offsets[k]
        return 1 + offsets.index(((n_chip - i) % n_chip, (n_col - j) % n_col))

    def block_rows(j, core_at):
        return rows_at((2 * j + core_at) * tl, tl)

    def size_of(i):
        return min(GROUP, hidden - i * GROUP)

    def w1_copy(i):
        return pltpu.make_async_copy(
            w1_hbm.at[:, pl.ds(i * GROUP, size_of(i))],
            w1.at[i, :, pl.ds(0, size_of(i))],
            w_sem.at[0, i],
        )

    def w2_copy(i):
        return pltpu.make_async_copy(
            w2_hbm.at[pl.ds(i * GROUP, size_of(i)), :],
            w2.at[i, pl.ds(0, size_of(i)), :],
            w_sem.at[1, i],
        )

    for i in range(groups):
        if size_of(i) < GROUP:
            w1[i, :, size_of(i):] = jnp.zeros((width, GROUP - size_of(i)), jnp.bfloat16)
            w2[i, size_of(i):, :] = jnp.zeros((GROUP - size_of(i), width), jnp.bfloat16)
        w1_copy(i).start()
    for i in range(groups):
        w2_copy(i).start()

    barrier = pltpu.get_barrier_semaphore()
    for k in range(near):
        chip_at, col_at = to_of(k)
        pl.semaphore_signal(
            barrier, inc=1, device_id=(2 * chip_at + core, row, col_at), device_id_type=MESH
        )
    pl.semaphore_signal(barrier, inc=1, device_id=(partner, row, col), device_id_type=MESH)

    @pl.when(row > 0)
    def _():
        pl.semaphore_signal(barrier, inc=1, device_id=(rep, row - 1, col), device_id_type=MESH)

    @pl.when(row < n_row - 1)
    def _():
        pl.semaphore_signal(barrier, inc=1, device_id=(rep, row + 1, col), device_id_type=MESH)

    at_ends = jnp.where(row > 0, 1, 0) + jnp.where(row < n_row - 1, 1, 0)
    pl.semaphore_wait(barrier, near + 1 + at_ends)

    def near_copy(which, source, target, k):
        chip_at, col_at = to_of(k)
        return pltpu.make_async_remote_copy(
            src_ref=source,
            dst_ref=target.at[block_rows(k + 1, core), :],
            send_sem=near_send.at[which, k],
            recv_sem=near_recv.at[which, k],
            device_id=(2 * chip_at + core, row, col_at),
            device_id_type=MESH,
        )

    def pair_copy(which, source, target, j):
        there = target.at[block_rows(j, core), :]
        return pltpu.make_async_remote_copy(
            src_ref=source if j == 0 else there,
            dst_ref=there,
            send_sem=pair_send.at[which, j],
            recv_sem=pair_recv.at[which, j],
            device_id=(partner, row, col),
            device_id_type=MESH,
        )

    def gather_start(which, source, target):
        pair_copy(which, source, target, 0).start()
        for k in range(near):
            near_copy(which, source, target, k).start()

    def gather_pass(which, source, target):
        for k in range(near):
            near_copy(which, source, target, k).wait_recv()
            pair_copy(which, source, target, k + 1).start()

    def gather_end(which, source, target):
        for j in range(1, near + 1):
            pair_copy(which, source, target, j).wait_recv()

    gather_start(0, x_ref, xa)
    xa[block_rows(0, core), :] = x_ref[...]
    counted = counts[0]
    for r in range(1, n_rep):
        counted = counted + counts[r]
    token_total = (MBT * counted).astype(jnp.float32)
    position = col * tl + lax.broadcasted_iota(jnp.int32, (tl, width), 0)
    kept = jnp.where(position < MBT * counts[rep], 1.0, 0.0)
    value = narrow(wide(cot_ref[...]) * kept / token_total)
    scaled[...] = value
    sa[block_rows(0, core), :] = value

    def place_units():
        flags = []
        for j in range(near + 1):
            chip_at, col_at = (chip, col) if j == 0 else from_of(j - 1)
            for core_at in range(2):
                for u in range(per_block):
                    batch = (col_at * tl + u * unit) // MBT
                    flags.append(jnp.where(batch < counts[2 * chip_at + core_at], 1, 0))
        total = flags[0]
        for flag in flags[1:]:
            total = total + flag
        before = 0 * total
        row_of = lax.broadcasted_iota(jnp.int32, (kept_rows, rows), 0)
        at_of = lax.broadcasted_iota(jnp.int32, (1, rows), 1)
        target = 0 * at_of
        kept_at = lax.broadcasted_iota(jnp.int32, (unit, kept_rows), 1)
        unit_at = lax.broadcasted_iota(jnp.int32, (unit, kept_rows), 0)
        for at, flag in enumerate(flags):
            first = unit * jnp.where(flag > 0, before, total + at - before)
            before = before + flag
            inside = jnp.logical_and(at_of >= at * unit, at_of < (at + 1) * unit)
            target = jnp.where(inside, first + at_of - at * unit, target)
            placed[at * unit:(at + 1) * unit, :] = narrow(
                jnp.where(kept_at == unit_at + first, 1.0, 0.0)
            )
        picked[...] = narrow(jnp.where(row_of == target, 1.0, 0.0))

    if pack:
        place_units()

    def kept_of(source, target):
        target[...] = narrow(product(picked[...], source[...]))

    places = (row, n_row - 1 - row)
    nexts = (row + 1, row - 1)
    furthest = jnp.maximum(row, n_row - 1 - row)
    pair = 2 if groups % 2 == 0 else 1
    part_runs = ((0, 0, 2 * tl, pair), (0, 2 * tl, rows, 1), (1, 0, kept_rows, 1))
    part_counts = (groups // pair, groups, groups)
    part_at = (0, groups // pair, groups // pair + groups)
    result_runs = ((0, 0, rows), (1, 0, kept_rows))
    result_tick = max(
        part_at[2] + groups,
        part_at[1] + (n_row - 1) * LAG + 1,
        part_at[2] + (n_row - 1) * LAG + 1 - groups,
    )
    use_tick = result_tick + (n_row - 1) * LAG
    ticks = use_tick + len(result_runs) * groups

    def part_copy(run, i, d):
        kind, low, high, many = part_runs[run]
        if many == 1:
            there = (i, d, pl.ds(low, high - low), slice(None))
        else:
            there = (pl.ds(i * many, many), d, pl.ds(low, high - low), slice(None))
        return pltpu.make_async_remote_copy(
            src_ref=part[kind].at[there],
            dst_ref=came[kind].at[there],
            send_sem=part_send.at[run, i, d],
            recv_sem=part_recv.at[run, i, d],
            device_id=(rep, nexts[d], col),
            device_id_type=MESH,
        )

    def result_copy(run, i, d):
        kind, low, high = result_runs[run]
        there = result[kind].at[i, 1 - d, pl.ds(low, high - low), :]
        return pltpu.make_async_remote_copy(
            src_ref=there,
            dst_ref=there,
            send_sem=res_send.at[run, i, d],
            recv_sem=res_recv.at[run, i, d],
            device_id=(rep, nexts[d], col),
            device_id_type=MESH,
        )

    def out_copy(kind, i, h):
        source = result_s if kind == 1 else packed if pack else result_h
        target = (act_hbm, grad_hbm)[kind]
        return pltpu.make_async_copy(
            source.at[i, h],
            target.at[:, pl.ds(pl.multiple_of(i * GROUP + h * HALF, HALF), HALF)],
            out_sem.at[kind, i, h],
        )

    def members(run, i, body):
        many = part_runs[run][3]
        for at in range(many):
            body(run, i * many + at)

    def make_part(run, i):
        kind, low, high, _ = part_runs[run]
        if kind == 0:
            value = product(xa[low:high, :], w1[i])
        else:
            value = right_product(sk[...], w2[i])
        value = narrow(value)
        part[kind][i, 0, low:high, :] = value[:, :HALF]
        part[kind][i, 1, low:high, :] = value[:, HALF:]

    def finish(run, i, d):
        kind, low, high, _ = part_runs[run]
        if kind == 0:
            total = wide(part_h[i, d, low:high, :]) + wide(came_h[i, d, low:high, :])
            result_h[i, d, low:high, :] = narrow(gelu_tanh(total))
        elif not pack:
            total = wide(part_h[i, d]) + wide(came_h[i, d])
            slope = wide(part_s[i, d]) + wide(came_s[i, d])
            result_s[i, d] = narrow(slope * gelu_slope(total))
        else:
            total = product(picked[...], part_h[i, d]) + product(picked[...], came_h[i, d])
            slope = wide(part_s[i, d]) + wide(came_s[i, d])
            result_s[i, d] = narrow(slope * gelu_slope(total))

    def add_up(kind, i):
        left = jnp.concatenate([result[kind][i, 0], result[kind][i, 1]], axis=1)
        more = product(left, w2[i]) if kind == 0 else right_product(left, w1[i])

        @pl.when(i == 0)
        def _():
            acc[kind][...] = more

        @pl.when(i > 0)
        def _():
            acc[kind][...] = acc[kind][...] + more

    def tick_part(run, d, i):
        kind, low, high, _ = part_runs[run]
        place = places[d]

        @pl.when(place > 0)
        def _():
            part_copy(run, i, d).wait_recv()

        @pl.when(jnp.logical_and(place > 0, place < n_row - 1))
        def _():
            def add(run, g):
                part[kind][g, d, low:high, :] = narrow(
                    wide(part[kind][g, d, low:high, :]) + wide(came[kind][g, d, low:high, :])
                )

            members(run, i, add)

        @pl.when(place < n_row - 1)
        def _():
            part_copy(run, i, d).start()

        @pl.when(place == n_row - 1)
        def _():
            members(run, i, lambda run, g: finish(run, g, d))

    def tick_result(run, d, i):
        @pl.when(places[d] > 0)
        def _():
            result_copy(run, i, d).wait_recv()

        @pl.when(places[d] < n_row - 1)
        def _():
            result_copy(run, i, d).start()

    def acc_rows(kind, j, core_at):
        if kind == 0 or not pack:
            return acc[kind][block_rows(j, core_at), :]
        return wide(back[block_rows(j, core_at), :])

    def unpack():
        back[...] = narrow(product(placed[...], narrow(acc_s[...])))

    def pair2_copy(kind):
        return pltpu.make_async_remote_copy(
            src_ref=pair_out.at[kind],
            dst_ref=pair_in.at[kind],
            send_sem=pair2_send.at[kind],
            recv_sem=pair2_recv.at[kind],
            device_id=(partner, row, col),
            device_id_type=MESH,
        )

    def chip_copy(k):
        chip_at, col_at = to_of(k)
        return pltpu.make_async_remote_copy(
            src_ref=chip_out.at[k],
            dst_ref=chip_in.at[k],
            send_sem=chip_send.at[k],
            recv_sem=chip_recv.at[k],
            device_id=(2 * chip_at + core, row, col_at),
            device_id_type=MESH,
        )

    def sum_start(kind):
        for j in range(near + 1):
            pair_out[kind, j * tl:(j + 1) * tl, :] = narrow(acc_rows(kind, j, 1 - core))
        pair2_copy(kind).start()

    def both_cores(kind, j):
        return acc_rows(kind, j, core) + wide(pair_in[kind, j * tl:(j + 1) * tl, :])

    def sum_pass():
        pair2_copy(0).wait_recv()
        for k in range(near):
            chip_out[k] = narrow(both_cores(0, block_to(k)))
            chip_copy(k).start()

    def sum_end():
        total = both_cores(0, 0)
        for k in range(near):
            chip_copy(k).wait_recv()
            total = total + wide(chip_in[k])
        bo_ref[...] = narrow(wide(x_ref[...]) + total)

    def out_start(kind, i):
        for h in range(2):
            @pl.when(2 * i + h < halves)
            def _():
                out_copy(kind, i, h).start()

    def pack_result(i):
        both = jnp.concatenate([result_h[i, 0], result_h[i, 1]], axis=1)
        both = narrow(product(picked[...], both))
        packed[i, 0] = both[:, :HALF]
        packed[i, 1] = both[:, HALF:]

    x_kept, s_kept = (xk, sk) if pack else (xa, sa)
    xk_out = pltpu.make_async_copy(x_kept, xk_hbm, out_sem.at[0, groups, 0])
    sk_out = pltpu.make_async_copy(s_kept, sk_hbm, out_sem.at[0, groups, 1])
    if not pack:
        sk = sa

    for i in range(pair):
        w1_copy(i).wait()
    pair_copy(0, x_ref, xa, 0).wait_recv()
    members(0, 0, make_part)

    def tick(t):
        for d in range(2):
            m = t - places[d] * LAG
            for run in range(len(part_runs)):
                i = m - part_at[run]

                @pl.when(jnp.logical_and(i >= 0, i < part_counts[run]))
                def _():
                    tick_part(run, d, i)

            for run in range(len(result_runs)):
                i = m - result_tick - run * groups

                @pl.when(jnp.logical_and(i >= 0, i < groups))
                def _():
                    tick_result(run, d, i)

        @pl.when(t == max(0, part_at[1] - 2))
        def _():
            gather_pass(0, x_ref, xa)
            gather_start(1, scaled, sa)

        @pl.when(t == part_at[1] - 1)
        def _():
            gather_end(0, x_ref, xa)

        @pl.when(t == part_at[1])
        def _():
            if pack:
                kept_of(xa, xk)
            xk_out.start()

        @pl.when(t == part_at[1] + groups // 2)
        def _():
            gather_pass(1, scaled, sa)

        @pl.when(t == part_at[2] - 1)
        def _():
            pair_copy(1, scaled, sa, 0).wait_recv()
            gather_end(1, scaled, sa)
            if pack:
                kept_of(sa, sk)
            for i in range(groups):
                w2_copy(i).wait()
            sk_out.start()

        for i in range(pair, groups):
            @pl.when(t == i // pair - 1)
            def _():
                w1_copy(i).wait()

        for run in range(len(part_runs)):
            i = t + 1 - part_at[run]

            @pl.when(jnp.logical_and(i >= 0, i < part_counts[run]))
            def _():
                members(run, i, make_part)

        for kind in range(2):
            i = t - result_tick - furthest * LAG - kind * groups

            @pl.when(jnp.logical_and(i >= 0, i < groups))
            def _():
                add_up(kind, i)
                if kind == 1:
                    out_start(1, i)
                    if pack:
                        pack_result(i)
                    out_start(0, i)

        @pl.when(t == use_tick + groups)
        def _():
            sum_start(0)

        @pl.when(t == use_tick + groups + 1)
        def _():
            sum_pass()

    each(ticks, tick)
    if pack:
        unpack()
    sum_start(1)
    sum_end()
    pair2_copy(1).wait_recv()
    base_ref[...] = wide(scaled[...]) + both_cores(1, 0)
    for k in range(near):
        sent_refs[k][...] = narrow(both_cores(1, block_to(k)))

    for which, source, target in ((0, x_ref, xa), (1, scaled, sa)):
        for k in range(near):
            near_copy(which, source, target, k).wait_send()
        for j in range(near + 1):
            pair_copy(which, source, target, j).wait_send()
    for kind in range(2):
        pair2_copy(kind).wait_send()
    for k in range(near):
        chip_copy(k).wait_send()
    xk_out.wait()
    sk_out.wait()

    def drain(i):
        for d in range(2):
            @pl.when(places[d] < n_row - 1)
            def _():
                for run in range(1, len(part_runs)):
                    part_copy(run, i, d).wait_send()
                for run in range(len(result_runs)):
                    result_copy(run, i, d).wait_send()

            @pl.when(jnp.logical_and(places[d] < n_row - 1, i < part_counts[0]))
            def _():
                part_copy(0, i, d).wait_send()

            for kind in range(2):
                @pl.when(2 * i + d < halves)
                def _():
                    out_copy(kind, i, d).wait()

    each(groups, drain)


def strip_of(size, most):
    return next(strip for strip in (512, 256, 128) if strip <= most and size % strip == 0)


def weight_grads(activated, scaled, tokens, hidden_grad, block_output):
    depth, hidden = activated.shape
    width = scaled.shape[1]
    high, low = strip_of(hidden, 512), strip_of(width, 512)
    cuts = 2 if hidden % (2 * HALF) == 0 else 1
    across = hidden // cuts
    first_jobs, second_jobs = hidden // high, width // low * cuts

    def kernel(
        a_hbm, s_hbm, x_hbm, g_hbm, b_hbm, out_grad, in_grad, b_out,
        a, s, x, g, b, first_slots, second_slots, in_sem, first_sem, second_sem, b_sem,
    ):
        def a_copy(i):
            columns = rows_at(i * high, high)
            return pltpu.make_async_copy(a_hbm.at[:, columns], a.at[:, columns], in_sem.at[3 + i])

        def first_out(i):
            slot = lax.rem(i, SLOTS)
            return pltpu.make_async_copy(
                first_slots.at[slot], out_grad.at[rows_at(i * high, high), :], first_sem.at[slot]
            )

        def second_out(i):
            slot = lax.rem(i, SLOTS)
            rows, columns = rows_at(i // cuts * low, low), rows_at(lax.rem(i, cuts) * across, across)
            return pltpu.make_async_copy(
                second_slots.at[slot], in_grad.at[rows, columns], second_sem.at[slot]
            )

        s_copy = pltpu.make_async_copy(s_hbm, s, in_sem.at[0])
        x_copy = pltpu.make_async_copy(x_hbm, x, in_sem.at[1])
        g_copy = pltpu.make_async_copy(g_hbm, g, in_sem.at[2])
        b_copy = pltpu.make_async_copy(b_hbm, b, b_sem.at[0])
        b_back = pltpu.make_async_copy(b, b_out, b_sem.at[1])
        s_copy.start()
        for i in range(first_jobs):
            a_copy(i).start()
        x_copy.start()
        g_copy.start()
        b_copy.start()
        s_copy.wait()

        def first(i):
            a_copy(i).wait()

            @pl.when(i >= SLOTS)
            def _():
                first_out(i - SLOTS).wait()

            left = a[:, rows_at(i * high, high)]
            first_slots[lax.rem(i, SLOTS)] = first_product(left, s[...])
            first_out(i).start()

        each(first_jobs, first)
        x_copy.wait()
        g_copy.wait()
        b_copy.wait()
        b_back.start()

        def second(i):
            @pl.when(i >= SLOTS)
            def _():
                second_out(i - SLOTS).wait()

            left = x[:, rows_at(i // cuts * low, low)]
            right = g[:, rows_at(lax.rem(i, cuts) * across, across)]
            second_slots[lax.rem(i, SLOTS)] = first_product(left, right)
            second_out(i).start()

        each(second_jobs, second)
        for i in range(max(0, first_jobs - SLOTS), first_jobs):
            first_out(i).wait()
        for i in range(max(0, second_jobs - SLOTS), second_jobs):
            second_out(i).wait()
        b_back.wait()

    anyw = pl.BlockSpec(memory_space=pl.ANY)
    bf16, f32 = jnp.bfloat16, jnp.float32
    return pl.pallas_call(
        kernel,
        in_specs=[anyw] * 5,
        out_specs=(anyw,) * 3,
        out_shape=(
            jax.ShapeDtypeStruct((hidden, width), f32),
            jax.ShapeDtypeStruct((width, hidden), f32),
            jax.ShapeDtypeStruct(block_output.shape, bf16),
        ),
        scratch_shapes=[
            pltpu.VMEM((depth, hidden), bf16),
            pltpu.VMEM((depth, width), bf16),
            pltpu.VMEM((depth, width), bf16),
            pltpu.VMEM((depth, hidden), bf16),
            pltpu.VMEM(block_output.shape, bf16),
            pltpu.VMEM((SLOTS, high, width), f32),
            pltpu.VMEM((SLOTS, low, across), f32),
            pltpu.SemaphoreType.DMA((3 + first_jobs,)),
            pltpu.SemaphoreType.DMA((SLOTS,)),
            pltpu.SemaphoreType.DMA((SLOTS,)),
            pltpu.SemaphoreType.DMA((2,)),
        ],
        compiler_params=pltpu.CompilerParams(vmem_limit_bytes=60_000_000),
        cost_estimate=pl.CostEstimate(
            flops=4 * hidden * depth * width,
            bytes_accessed=8 * hidden * width + 4 * depth * (hidden + width),
            transcendentals=0,
        ),
    )(activated, scaled, tokens, hidden_grad, block_output)


def step(sizes, number, counts, inputs, cotangent, w_in, w_out):
    n_rep, n_row, n_col, tl, width, hidden, groups, rows, kept_rows = sizes
    blocks = n_rep * n_col // 2
    near = blocks - 1
    pack = kept_rows < rows
    spare = kept_rows if pack else 16
    bf16, f32 = jnp.bfloat16, jnp.float32
    vmem = pl.BlockSpec(memory_space=pltpu.VMEM)
    anyw = pl.BlockSpec(memory_space=pl.ANY)
    dma = pltpu.SemaphoreType.DMA
    block_output, activated, hidden_grad, tokens_kept, scaled_kept, base, *sent = pl.pallas_call(
        functools.partial(step_kernel, sizes),
        out_shape=(
            jax.ShapeDtypeStruct((tl, width), bf16),
            jax.ShapeDtypeStruct((kept_rows, hidden), bf16),
            jax.ShapeDtypeStruct((kept_rows, hidden), bf16),
            jax.ShapeDtypeStruct((kept_rows, width), bf16),
            jax.ShapeDtypeStruct((kept_rows, width), bf16),
            jax.ShapeDtypeStruct((tl, width), f32),
            *[jax.ShapeDtypeStruct((tl, width), bf16)] * near,
        ),
        in_specs=[pl.BlockSpec(memory_space=pltpu.SMEM), vmem, vmem, anyw, anyw],
        out_specs=(vmem, anyw, anyw, anyw, anyw, vmem, *[vmem] * near),
        scratch_shapes=[
            pltpu.VMEM((groups, width, GROUP), bf16),
            pltpu.VMEM((groups, GROUP, width), bf16),
            pltpu.VMEM((rows, width), bf16),
            pltpu.VMEM((rows, width), bf16),
            pltpu.VMEM((tl, width), bf16),
            pltpu.VMEM((spare, width), bf16),
            pltpu.VMEM((spare, width), bf16),
            pltpu.VMEM((spare, rows), bf16),
            pltpu.VMEM((rows, spare), bf16),
            pltpu.VMEM((rows if pack else 16, width), bf16),
            pltpu.VMEM((groups, 2, rows, HALF), bf16),
            pltpu.VMEM((groups, 2, kept_rows, HALF), bf16),
            pltpu.VMEM((groups, 2, rows, HALF), bf16),
            pltpu.VMEM((groups, 2, kept_rows, HALF), bf16),
            pltpu.VMEM((groups, 2, rows, HALF), bf16),
            pltpu.VMEM((groups, 2, kept_rows, HALF), bf16),
            pltpu.VMEM((groups, 2, spare, HALF), bf16),
            pltpu.VMEM((rows, width), f32),
            pltpu.VMEM((kept_rows, width), f32),
            pltpu.VMEM((2, blocks * tl, width), bf16),
            pltpu.VMEM((2, blocks * tl, width), bf16),
            pltpu.VMEM((near, tl, width), bf16),
            pltpu.VMEM((near, tl, width), bf16),
            dma((2, groups)),
            dma((2, near)),
            dma((2, near)),
            dma((2, near + 1)),
            dma((2, near + 1)),
            dma((3, groups, 2)),
            dma((3, groups, 2)),
            dma((2, groups, 2)),
            dma((2, groups, 2)),
            dma((2, groups + 1, 2)),
            dma((2,)),
            dma((2,)),
            dma((near,)),
            dma((near,)),
        ],
        compiler_params=pltpu.CompilerParams(
            collective_id=number, has_side_effects=True, vmem_limit_bytes=67_000_000
        ),
    )(counts, inputs, cotangent, w_in, w_out)
    n_chip = n_rep // 2
    total = base
    for (i, j), own in zip(distances(n_chip, n_col), sent):
        pairs = [
            (
                (2 * chip + core) * n_col + col,
                (2 * ((chip + i) % n_chip) + core) * n_col + (col + j) % n_col,
            )
            for chip in range(n_chip) for core in range(2) for col in range(n_col)
        ]
        total = total + wide(lax.ppermute(own, ("rep", "col"), pairs))
    w_out_grad, w_in_grad, block_output = weight_grads(
        activated, scaled_kept, tokens_kept, hidden_grad, block_output
    )
    return block_output, narrow(total), w_in_grad, w_out_grad


def body(inputs, w_in, w_out, cotangent, counts):
    tl, width = inputs.shape[1], inputs.shape[2]
    hidden = w_in.shape[1]
    n_rep, n_row, n_col = (lax.axis_size(name) for name in ("rep", "row", "col"))
    rows = n_rep * n_col * tl
    cases = [rows * eighths // 8 for eighths in EIGHTHS]
    sizes = (n_rep, n_row, n_col, tl, width, hidden, -(-hidden // GROUP), rows)
    kept_rows = MBT * jnp.sum(counts)
    case = sum((kept_rows > rows_of_case).astype(jnp.int32) for rows_of_case in cases[:-1])
    args = (
        counts, inputs.reshape(tl, width), cotangent.reshape(tl, width), w_in, w_out
    )
    branches = [
        functools.partial(step, (*sizes, kept), number) for number, kept in enumerate(cases)
    ]
    if len(branches) == 1:
        block_output, input_grad, w_in_grad, w_out_grad = branches[0](*args)
    else:
        block_output, input_grad, w_in_grad, w_out_grad = lax.switch(case, branches, *args)
    return (
        block_output.reshape(1, tl, width),
        input_grad.reshape(1, tl, width),
        w_in_grad,
        w_out_grad,
    )


def solution(mesh):
    placed = (
        P("rep", "col", "row"),
        P("row", ("rep", "col")),
        P(("rep", "col"), "row"),
        P("rep", "col", "row"),
        P(),
    )
    return jax.shard_map(
        body,
        mesh=mesh,
        in_specs=placed,
        out_specs=(
            P("rep", "col", "row"),
            P("rep", "col", "row"),
            P("row", ("rep", "col")),
            P(("rep", "col"), "row"),
        ),
        check_vma=False,
    )
```

```python
import functools

import jax
import jax.numpy as jnp
from jax import lax
from jax.experimental import pallas as pl
from jax.experimental.pallas import tpu as pltpu
from jax.sharding import PartitionSpec as P

MBT = 32
HALF = 128
GROUP = 2 * HALF
LAG = 3
SLOTS = 3
EIGHTHS = (4, 5, 6, 8)
MESH = pl.DeviceIdType.MESH

root_coef = 0.7978845608028654
cubic_coef = 0.044715


def gelu_tanh(values):
    inner = root_coef * (values + cubic_coef * values * values * values)
    return 0.5 * values * (1.0 + jnp.tanh(inner))


def gelu_slope(values):
    inner = root_coef * (values + cubic_coef * values * values * values)
    tangent = jnp.tanh(inner)
    return 0.5 * (1.0 + tangent) + 0.5 * values * (1.0 - tangent * tangent) * root_coef * (
        1.0 + 3.0 * cubic_coef * values * values
    )


def wide(values):
    return values.astype(jnp.float32)


def narrow(values):
    return values.astype(jnp.bfloat16)


def product(left, right):
    return jnp.dot(left, right, preferred_element_type=jnp.float32)


def right_product(left, right):
    return lax.dot_general(
        left, right, (((1,), (1,)), ((), ())), preferred_element_type=jnp.float32
    )


def first_product(left, right):
    return lax.dot_general(
        left, right, (((0,), (0,)), ((), ())), preferred_element_type=jnp.float32
    )


def rows_at(start, size):
    return pl.ds(pl.multiple_of(start, size), size)


def each(count, body):
    lax.fori_loop(0, count, lambda i, c: (body(i), c)[1], 0)


def distances(n_chip, n_col):
    return [(i, j) for i in range(n_chip) for j in range(n_col) if i + j > 0]


def step_kernel(
    sizes,
    counts, x_ref, cot_ref, w1_hbm, w2_hbm,
    bo_ref, act_hbm, grad_hbm, xk_hbm, sk_hbm, base_ref, *others,
):
    n_rep, n_row, n_col, tl, width, hidden, groups, rows, kept_rows = sizes
    near = n_rep * n_col // 2 - 1
    sent_refs, scratch = others[:near], others[near:]
    (
    w1, w2, xa, sa, scaled, xk, sk, picked, placed, back,
    part_h, part_s, came_h, came_s, result_h, result_s, packed,
    acc_h, acc_s, pair_out, pair_in, chip_out, chip_in,
    w_sem, near_send, near_recv, pair_send, pair_recv,
    part_send, part_recv, res_send, res_recv, out_sem,
    pair2_send, pair2_recv, chip_send, chip_recv,
    ) = scratch
    halves = hidden // HALF
    pack = kept_rows < rows
    unit = min(tl, MBT)
    per_block = tl // unit
    rep, row, col = (lax.axis_index(name) for name in ("rep", "row", "col"))
    core, chip = lax.rem(rep, 2), rep // 2
    n_chip = n_rep // 2
    partner = rep + 1 - 2 * core
    offsets = distances(n_chip, n_col)
    part, came = (part_h, part_s), (came_h, came_s)
    result, acc = (result_h, result_s), (acc_h, acc_s)

    def to_of(k):
        i, j = offsets[k]
        return lax.rem(chip + i, n_chip), lax.rem(col + j, n_col)

    def from_of(k):
        i, j = offsets[k]
        return lax.rem(chip + n_chip - i, n_chip), lax.rem(col + n_col - j, n_col)

    def block_to(k):
        i, j = offsets[k]
        return 1 + offsets.index(((n_chip - i) % n_chip, (n_col - j) % n_col))

    def block_rows(j, core_at):
        return rows_at((2 * j + core_at) * tl, tl)

    def size_of(i):
        return min(GROUP, hidden - i * GROUP)

    def w1_copy(i):
        return pltpu.make_async_copy(
            w1_hbm.at[:, pl.ds(i * GROUP, size_of(i))],
            w1.at[i, :, pl.ds(0, size_of(i))],
            w_sem.at[0, i],
        )

    def w2_copy(i):
        return pltpu.make_async_copy(
            w2_hbm.at[pl.ds(i * GROUP, size_of(i)), :],
            w2.at[i, pl.ds(0, size_of(i)), :],
            w_sem.at[1, i],
        )

    for i in range(groups):
        if size_of(i) < GROUP:
            w1[i, :, size_of(i):] = jnp.zeros((width, GROUP - size_of(i)), jnp.bfloat16)
            w2[i, size_of(i):, :] = jnp.zeros((GROUP - size_of(i), width), jnp.bfloat16)
        w1_copy(i).start()
    for i in range(groups):
        w2_copy(i).start()

    barrier = pltpu.get_barrier_semaphore()
    for k in range(near):
        chip_at, col_at = to_of(k)
        pl.semaphore_signal(
            barrier, inc=1, device_id=(2 * chip_at + core, row, col_at), device_id_type=MESH
        )
    pl.semaphore_signal(barrier, inc=1, device_id=(partner, row, col), device_id_type=MESH)

    @pl.when(row > 0)
    def _():
        pl.semaphore_signal(barrier, inc=1, device_id=(rep, row - 1, col), device_id_type=MESH)

    @pl.when(row < n_row - 1)
    def _():
        pl.semaphore_signal(barrier, inc=1, device_id=(rep, row + 1, col), device_id_type=MESH)

    at_ends = jnp.where(row > 0, 1, 0) + jnp.where(row < n_row - 1, 1, 0)
    pl.semaphore_wait(barrier, near + 1 + at_ends)

    def near_copy(which, source, target, k):
        chip_at, col_at = to_of(k)
        return pltpu.make_async_remote_copy(
            src_ref=source,
            dst_ref=target.at[block_rows(k + 1, core), :],
            send_sem=near_send.at[which, k],
            recv_sem=near_recv.at[which, k],
            device_id=(2 * chip_at + core, row, col_at),
            device_id_type=MESH,
        )

    def pair_copy(which, source, target, j):
        there = target.at[block_rows(j, core), :]
        return pltpu.make_async_remote_copy(
            src_ref=source if j == 0 else there,
            dst_ref=there,
            send_sem=pair_send.at[which, j],
            recv_sem=pair_recv.at[which, j],
            device_id=(partner, row, col),
            device_id_type=MESH,
        )

    def gather_start(which, source, target):
        pair_copy(which, source, target, 0).start()
        for k in range(near):
            near_copy(which, source, target, k).start()

    def gather_pass(which, source, target):
        for k in range(near):
            near_copy(which, source, target, k).wait_recv()
            pair_copy(which, source, target, k + 1).start()

    def gather_end(which, source, target):
        for j in range(1, near + 1):
            pair_copy(which, source, target, j).wait_recv()

    gather_start(0, x_ref, xa)
    xa[block_rows(0, core), :] = x_ref[...]
    counted = counts[0]
    for r in range(1, n_rep):
        counted = counted + counts[r]
    token_total = (MBT * counted).astype(jnp.float32)
    position = col * tl + lax.broadcasted_iota(jnp.int32, (tl, width), 0)
    kept = jnp.where(position < MBT * counts[rep], 1.0, 0.0)
    value = narrow(wide(cot_ref[...]) * kept / token_total)
    scaled[...] = value
    sa[block_rows(0, core), :] = value

    def place_units():
        flags = []
        for j in range(near + 1):
            chip_at, col_at = (chip, col) if j == 0 else from_of(j - 1)
            for core_at in range(2):
                for u in range(per_block):
                    batch = (col_at * tl + u * unit) // MBT
                    flags.append(jnp.where(batch < counts[2 * chip_at + core_at], 1, 0))
        total = flags[0]
        for flag in flags[1:]:
            total = total + flag
        before = 0 * total
        row_of = lax.broadcasted_iota(jnp.int32, (kept_rows, rows), 0)
        at_of = lax.broadcasted_iota(jnp.int32, (1, rows), 1)
        target = 0 * at_of
        kept_at = lax.broadcasted_iota(jnp.int32, (unit, kept_rows), 1)
        unit_at = lax.broadcasted_iota(jnp.int32, (unit, kept_rows), 0)
        for at, flag in enumerate(flags):
            first = unit * jnp.where(flag > 0, before, total + at - before)
            before = before + flag
            inside = jnp.logical_and(at_of >= at * unit, at_of < (at + 1) * unit)
            target = jnp.where(inside, first + at_of - at * unit, target)
            placed[at * unit:(at + 1) * unit, :] = narrow(
                jnp.where(kept_at == unit_at + first, 1.0, 0.0)
            )
        picked[...] = narrow(jnp.where(row_of == target, 1.0, 0.0))

    if pack:
        place_units()

    def kept_of(source, target):
        target[...] = narrow(product(picked[...], source[...]))

    places = (row, n_row - 1 - row)
    nexts = (row + 1, row - 1)
    furthest = jnp.maximum(row, n_row - 1 - row)
    pair = 2 if groups % 2 == 0 else 1
    part_runs = ((0, 0, 2 * tl, pair), (0, 2 * tl, rows, 1), (1, 0, kept_rows, 1))
    part_counts = (groups // pair, groups, groups)
    part_at = (0, groups // pair, groups // pair + groups)
    result_runs = ((0, 0, rows), (1, 0, kept_rows))
    result_tick = max(
        part_at[2] + groups,
        part_at[1] + (n_row - 1) * LAG + 1,
        part_at[2] + (n_row - 1) * LAG + 1 - groups,
    )
    use_tick = result_tick + (n_row - 1) * LAG
    ticks = use_tick + len(result_runs) * groups

    def part_copy(run, i, d):
        kind, low, high, many = part_runs[run]
        if many == 1:
            there = (i, d, pl.ds(low, high - low), slice(None))
        else:
            there = (pl.ds(i * many, many), d, pl.ds(low, high - low), slice(None))
        return pltpu.make_async_remote_copy(
            src_ref=part[kind].at[there],
            dst_ref=came[kind].at[there],
            send_sem=part_send.at[run, i, d],
            recv_sem=part_recv.at[run, i, d],
            device_id=(rep, nexts[d], col),
            device_id_type=MESH,
        )

    def result_copy(run, i, d):
        kind, low, high = result_runs[run]
        there = result[kind].at[i, 1 - d, pl.ds(low, high - low), :]
        return pltpu.make_async_remote_copy(
            src_ref=there,
            dst_ref=there,
            send_sem=res_send.at[run, i, d],
            recv_sem=res_recv.at[run, i, d],
            device_id=(rep, nexts[d], col),
            device_id_type=MESH,
        )

    def out_copy(kind, i, h):
        source = result_s if kind == 1 else packed if pack else result_h
        target = (act_hbm, grad_hbm)[kind]
        return pltpu.make_async_copy(
            source.at[i, h],
            target.at[:, pl.ds(pl.multiple_of(i * GROUP + h * HALF, HALF), HALF)],
            out_sem.at[kind, i, h],
        )

    def members(run, i, body):
        many = part_runs[run][3]
        for at in range(many):
            body(run, i * many + at)

    def make_part(run, i):
        kind, low, high, _ = part_runs[run]
        if kind == 0:
            value = product(xa[low:high, :], w1[i])
        else:
            value = right_product(sk[...], w2[i])
        value = narrow(value)
        part[kind][i, 0, low:high, :] = value[:, :HALF]
        part[kind][i, 1, low:high, :] = value[:, HALF:]

    def finish(run, i, d):
        kind, low, high, _ = part_runs[run]
        if kind == 0:
            total = wide(part_h[i, d, low:high, :]) + wide(came_h[i, d, low:high, :])
            result_h[i, d, low:high, :] = narrow(gelu_tanh(total))
        elif not pack:
            total = wide(part_h[i, d]) + wide(came_h[i, d])
            slope = wide(part_s[i, d]) + wide(came_s[i, d])
            result_s[i, d] = narrow(slope * gelu_slope(total))
        else:
            total = product(picked[...], part_h[i, d]) + product(picked[...], came_h[i, d])
            slope = wide(part_s[i, d]) + wide(came_s[i, d])
            result_s[i, d] = narrow(slope * gelu_slope(total))

    def add_up(kind, i):
        left = jnp.concatenate([result[kind][i, 0], result[kind][i, 1]], axis=1)
        more = product(left, w2[i]) if kind == 0 else right_product(left, w1[i])

        @pl.when(i == 0)
        def _():
            acc[kind][...] = more

        @pl.when(i > 0)
        def _():
            acc[kind][...] = acc[kind][...] + more

    def tick_part(run, d, i):
        kind, low, high, _ = part_runs[run]
        place = places[d]

        @pl.when(place > 0)
        def _():
            part_copy(run, i, d).wait_recv()

        @pl.when(jnp.logical_and(place > 0, place < n_row - 1))
        def _():
            def add(run, g):
                part[kind][g, d, low:high, :] = narrow(
                    wide(part[kind][g, d, low:high, :]) + wide(came[kind][g, d, low:high, :])
                )

            members(run, i, add)

        @pl.when(place < n_row - 1)
        def _():
            part_copy(run, i, d).start()

        @pl.when(place == n_row - 1)
        def _():
            members(run, i, lambda run, g: finish(run, g, d))

    def tick_result(run, d, i):
        @pl.when(places[d] > 0)
        def _():
            result_copy(run, i, d).wait_recv()

        @pl.when(places[d] < n_row - 1)
        def _():
            result_copy(run, i, d).start()

    def acc_rows(kind, j, core_at):
        if kind == 0 or not pack:
            return acc[kind][block_rows(j, core_at), :]
        return wide(back[block_rows(j, core_at), :])

    def unpack():
        back[...] = narrow(product(placed[...], narrow(acc_s[...])))

    def pair2_copy(kind):
        return pltpu.make_async_remote_copy(
            src_ref=pair_out.at[kind],
            dst_ref=pair_in.at[kind],
            send_sem=pair2_send.at[kind],
            recv_sem=pair2_recv.at[kind],
            device_id=(partner, row, col),
            device_id_type=MESH,
        )

    def chip_copy(k):
        chip_at, col_at = to_of(k)
        return pltpu.make_async_remote_copy(
            src_ref=chip_out.at[k],
            dst_ref=chip_in.at[k],
            send_sem=chip_send.at[k],
            recv_sem=chip_recv.at[k],
            device_id=(2 * chip_at + core, row, col_at),
            device_id_type=MESH,
        )

    def sum_start(kind):
        for j in range(near + 1):
            pair_out[kind, j * tl:(j + 1) * tl, :] = narrow(acc_rows(kind, j, 1 - core))
        pair2_copy(kind).start()

    def both_cores(kind, j):
        return acc_rows(kind, j, core) + wide(pair_in[kind, j * tl:(j + 1) * tl, :])

    def sum_pass():
        pair2_copy(0).wait_recv()
        for k in range(near):
            chip_out[k] = narrow(both_cores(0, block_to(k)))
            chip_copy(k).start()

    def sum_end():
        total = both_cores(0, 0)
        for k in range(near):
            chip_copy(k).wait_recv()
            total = total + wide(chip_in[k])
        bo_ref[...] = narrow(wide(x_ref[...]) + total)

    def out_start(kind, i):
        for h in range(2):
            @pl.when(2 * i + h < halves)
            def _():
                out_copy(kind, i, h).start()

    def pack_result(i):
        both = jnp.concatenate([result_h[i, 0], result_h[i, 1]], axis=1)
        both = narrow(product(picked[...], both))
        packed[i, 0] = both[:, :HALF]
        packed[i, 1] = both[:, HALF:]

    x_kept, s_kept = (xk, sk) if pack else (xa, sa)
    xk_out = pltpu.make_async_copy(x_kept, xk_hbm, out_sem.at[0, groups, 0])
    sk_out = pltpu.make_async_copy(s_kept, sk_hbm, out_sem.at[0, groups, 1])
    if not pack:
        sk = sa

    for i in range(pair):
        w1_copy(i).wait()
    pair_copy(0, x_ref, xa, 0).wait_recv()
    members(0, 0, make_part)

    def tick(t):
        for d in range(2):
            m = t - places[d] * LAG
            for run in range(len(part_runs)):
                i = m - part_at[run]

                @pl.when(jnp.logical_and(i >= 0, i < part_counts[run]))
                def _():
                    tick_part(run, d, i)

            for run in range(len(result_runs)):
                i = m - result_tick - run * groups

                @pl.when(jnp.logical_and(i >= 0, i < groups))
                def _():
                    tick_result(run, d, i)

        @pl.when(t == max(0, part_at[1] - 2))
        def _():
            gather_pass(0, x_ref, xa)
            gather_start(1, scaled, sa)

        @pl.when(t == part_at[1] - 1)
        def _():
            gather_end(0, x_ref, xa)

        @pl.when(t == part_at[1])
        def _():
            if pack:
                kept_of(xa, xk)
            xk_out.start()

        @pl.when(t == part_at[1] + groups // 2)
        def _():
            gather_pass(1, scaled, sa)

        @pl.when(t == part_at[2] - 1)
        def _():
            pair_copy(1, scaled, sa, 0).wait_recv()
            gather_end(1, scaled, sa)
            if pack:
                kept_of(sa, sk)
            for i in range(groups):
                w2_copy(i).wait()
            sk_out.start()

        for i in range(pair, groups):
            @pl.when(t == i // pair - 1)
            def _():
                w1_copy(i).wait()

        for run in range(len(part_runs)):
            i = t + 1 - part_at[run]

            @pl.when(jnp.logical_and(i >= 0, i < part_counts[run]))
            def _():
                members(run, i, make_part)

        for kind in range(2):
            i = t - result_tick - furthest * LAG - kind * groups

            @pl.when(jnp.logical_and(i >= 0, i < groups))
            def _():
                add_up(kind, i)
                if kind == 1:
                    out_start(1, i)
                    if pack:
                        pack_result(i)
                    out_start(0, i)

        @pl.when(t == use_tick + groups)
        def _():
            sum_start(0)

        @pl.when(t == use_tick + groups + 1)
        def _():
            sum_pass()

    each(ticks, tick)
    if pack:
        unpack()
    sum_start(1)
    sum_end()
    pair2_copy(1).wait_recv()
    base_ref[...] = wide(scaled[...]) + both_cores(1, 0)
    for k in range(near):
        sent_refs[k][...] = narrow(both_cores(1, block_to(k)))

    for which, source, target in ((0, x_ref, xa), (1, scaled, sa)):
        for k in range(near):
            near_copy(which, source, target, k).wait_send()
        for j in range(near + 1):
            pair_copy(which, source, target, j).wait_send()
    for kind in range(2):
        pair2_copy(kind).wait_send()
    for k in range(near):
        chip_copy(k).wait_send()
    xk_out.wait()
    sk_out.wait()

    def drain(i):
        for d in range(2):
            @pl.when(places[d] < n_row - 1)
            def _():
                for run in range(1, len(part_runs)):
                    part_copy(run, i, d).wait_send()
                for run in range(len(result_runs)):
                    result_copy(run, i, d).wait_send()

            @pl.when(jnp.logical_and(places[d] < n_row - 1, i < part_counts[0]))
            def _():
                part_copy(0, i, d).wait_send()

            for kind in range(2):
                @pl.when(2 * i + d < halves)
                def _():
                    out_copy(kind, i, d).wait()

    each(groups, drain)


def strip_of(size, most):
    return next(strip for strip in (512, 256, 128) if strip <= most and size % strip == 0)


def weight_grads(activated, scaled, tokens, hidden_grad, block_output):
    depth, hidden = activated.shape
    width = scaled.shape[1]
    high, low = strip_of(hidden, 512), strip_of(width, 512)
    cuts = 2 if hidden % (2 * HALF) == 0 else 1
    across = hidden // cuts
    first_jobs, second_jobs = hidden // high, width // low * cuts

    def kernel(
        a_hbm, s_hbm, x_hbm, g_hbm, b_hbm, out_grad, in_grad, b_out,
        a, s, x, g, b, first_slots, second_slots, in_sem, first_sem, second_sem, b_sem,
    ):
        def a_copy(i):
            columns = rows_at(i * high, high)
            return pltpu.make_async_copy(a_hbm.at[:, columns], a.at[:, columns], in_sem.at[3 + i])

        def first_out(i):
            slot = lax.rem(i, SLOTS)
            return pltpu.make_async_copy(
                first_slots.at[slot], out_grad.at[rows_at(i * high, high), :], first_sem.at[slot]
            )

        def second_out(i):
            slot = lax.rem(i, SLOTS)
            rows, columns = rows_at(i // cuts * low, low), rows_at(lax.rem(i, cuts) * across, across)
            return pltpu.make_async_copy(
                second_slots.at[slot], in_grad.at[rows, columns], second_sem.at[slot]
            )

        s_copy = pltpu.make_async_copy(s_hbm, s, in_sem.at[0])
        x_copy = pltpu.make_async_copy(x_hbm, x, in_sem.at[1])
        g_copy = pltpu.make_async_copy(g_hbm, g, in_sem.at[2])
        b_copy = pltpu.make_async_copy(b_hbm, b, b_sem.at[0])
        b_back = pltpu.make_async_copy(b, b_out, b_sem.at[1])
        s_copy.start()
        for i in range(first_jobs):
            a_copy(i).start()
        x_copy.start()
        g_copy.start()
        b_copy.start()
        s_copy.wait()

        def first(i):
            a_copy(i).wait()

            @pl.when(i >= SLOTS)
            def _():
                first_out(i - SLOTS).wait()

            left = a[:, rows_at(i * high, high)]
            first_slots[lax.rem(i, SLOTS)] = first_product(left, s[...])
            first_out(i).start()

        each(first_jobs, first)
        x_copy.wait()
        g_copy.wait()
        b_copy.wait()
        b_back.start()

        def second(i):
            @pl.when(i >= SLOTS)
            def _():
                second_out(i - SLOTS).wait()

            left = x[:, rows_at(i // cuts * low, low)]
            right = g[:, rows_at(lax.rem(i, cuts) * across, across)]
            second_slots[lax.rem(i, SLOTS)] = first_product(left, right)
            second_out(i).start()

        each(second_jobs, second)
        for i in range(max(0, first_jobs - SLOTS), first_jobs):
            first_out(i).wait()
        for i in range(max(0, second_jobs - SLOTS), second_jobs):
            second_out(i).wait()
        b_back.wait()

    anyw = pl.BlockSpec(memory_space=pl.ANY)
    bf16, f32 = jnp.bfloat16, jnp.float32
    return pl.pallas_call(
        kernel,
        in_specs=[anyw] * 5,
        out_specs=(anyw,) * 3,
        out_shape=(
            jax.ShapeDtypeStruct((hidden, width), f32),
            jax.ShapeDtypeStruct((width, hidden), f32),
            jax.ShapeDtypeStruct(block_output.shape, bf16),
        ),
        scratch_shapes=[
            pltpu.VMEM((depth, hidden), bf16),
            pltpu.VMEM((depth, width), bf16),
            pltpu.VMEM((depth, width), bf16),
            pltpu.VMEM((depth, hidden), bf16),
            pltpu.VMEM(block_output.shape, bf16),
            pltpu.VMEM((SLOTS, high, width), f32),
            pltpu.VMEM((SLOTS, low, across), f32),
            pltpu.SemaphoreType.DMA((3 + first_jobs,)),
            pltpu.SemaphoreType.DMA((SLOTS,)),
            pltpu.SemaphoreType.DMA((SLOTS,)),
            pltpu.SemaphoreType.DMA((2,)),
        ],
        compiler_params=pltpu.CompilerParams(vmem_limit_bytes=60_000_000),
        cost_estimate=pl.CostEstimate(
            flops=4 * hidden * depth * width,
            bytes_accessed=8 * hidden * width + 4 * depth * (hidden + width),
            transcendentals=0,
        ),
    )(activated, scaled, tokens, hidden_grad, block_output)


def step(sizes, number, counts, inputs, cotangent, w_in, w_out):
    n_rep, n_row, n_col, tl, width, hidden, groups, rows, kept_rows = sizes
    blocks = n_rep * n_col // 2
    near = blocks - 1
    pack = kept_rows < rows
    spare = kept_rows if pack else 16
    bf16, f32 = jnp.bfloat16, jnp.float32
    vmem = pl.BlockSpec(memory_space=pltpu.VMEM)
    anyw = pl.BlockSpec(memory_space=pl.ANY)
    dma = pltpu.SemaphoreType.DMA
    block_output, activated, hidden_grad, tokens_kept, scaled_kept, base, *sent = pl.pallas_call(
        functools.partial(step_kernel, sizes),
        out_shape=(
            jax.ShapeDtypeStruct((tl, width), bf16),
            jax.ShapeDtypeStruct((kept_rows, hidden), bf16),
            jax.ShapeDtypeStruct((kept_rows, hidden), bf16),
            jax.ShapeDtypeStruct((kept_rows, width), bf16),
            jax.ShapeDtypeStruct((kept_rows, width), bf16),
            jax.ShapeDtypeStruct((tl, width), f32),
            *[jax.ShapeDtypeStruct((tl, width), bf16)] * near,
        ),
        in_specs=[pl.BlockSpec(memory_space=pltpu.SMEM), vmem, vmem, anyw, anyw],
        out_specs=(vmem, anyw, anyw, anyw, anyw, vmem, *[vmem] * near),
        scratch_shapes=[
            pltpu.VMEM((groups, width, GROUP), bf16),
            pltpu.VMEM((groups, GROUP, width), bf16),
            pltpu.VMEM((rows, width), bf16),
            pltpu.VMEM((rows, width), bf16),
            pltpu.VMEM((tl, width), bf16),
            pltpu.VMEM((spare, width), bf16),
            pltpu.VMEM((spare, width), bf16),
            pltpu.VMEM((spare, rows), bf16),
            pltpu.VMEM((rows, spare), bf16),
            pltpu.VMEM((rows if pack else 16, width), bf16),
            pltpu.VMEM((groups, 2, rows, HALF), bf16),
            pltpu.VMEM((groups, 2, kept_rows, HALF), bf16),
            pltpu.VMEM((groups, 2, rows, HALF), bf16),
            pltpu.VMEM((groups, 2, kept_rows, HALF), bf16),
            pltpu.VMEM((groups, 2, rows, HALF), bf16),
            pltpu.VMEM((groups, 2, kept_rows, HALF), bf16),
            pltpu.VMEM((groups, 2, spare, HALF), bf16),
            pltpu.VMEM((rows, width), f32),
            pltpu.VMEM((kept_rows, width), f32),
            pltpu.VMEM((2, blocks * tl, width), bf16),
            pltpu.VMEM((2, blocks * tl, width), bf16),
            pltpu.VMEM((near, tl, width), bf16),
            pltpu.VMEM((near, tl, width), bf16),
            dma((2, groups)),
            dma((2, near)),
            dma((2, near)),
            dma((2, near + 1)),
            dma((2, near + 1)),
            dma((3, groups, 2)),
            dma((3, groups, 2)),
            dma((2, groups, 2)),
            dma((2, groups, 2)),
            dma((2, groups + 1, 2)),
            dma((2,)),
            dma((2,)),
            dma((near,)),
            dma((near,)),
        ],
        compiler_params=pltpu.CompilerParams(
            collective_id=number, has_side_effects=True, vmem_limit_bytes=67_000_000
        ),
    )(counts, inputs, cotangent, w_in, w_out)
    n_chip = n_rep // 2
    total = base
    for (i, j), own in zip(distances(n_chip, n_col), sent):
        pairs = [
            (
                (2 * chip + core) * n_col + col,
                (2 * ((chip + i) % n_chip) + core) * n_col + (col + j) % n_col,
            )
            for chip in range(n_chip) for core in range(2) for col in range(n_col)
        ]
        total = total + wide(lax.ppermute(own, ("rep", "col"), pairs))
    w_out_grad, w_in_grad, block_output = weight_grads(
        activated, scaled_kept, tokens_kept, hidden_grad, block_output
    )
    return block_output, narrow(total), w_in_grad, w_out_grad


def body(inputs, w_in, w_out, cotangent, counts):
    tl, width = inputs.shape[1], inputs.shape[2]
    hidden = w_in.shape[1]
    n_rep, n_row, n_col = (lax.axis_size(name) for name in ("rep", "row", "col"))
    rows = n_rep * n_col * tl
    cases = [rows * eighths // 8 for eighths in EIGHTHS]
    sizes = (n_rep, n_row, n_col, tl, width, hidden, -(-hidden // GROUP), rows)
    counted = counts[0]
    for r in range(1, n_rep):
        counted = counted + counts[r]
    kept_rows = MBT * counted
    case = sum((kept_rows > rows_of_case).astype(jnp.int32) for rows_of_case in cases[:-1])
    args = (
        counts, inputs.reshape(tl, width), cotangent.reshape(tl, width), w_in, w_out
    )
    branches = [
        functools.partial(step, (*sizes, kept), number) for number, kept in enumerate(cases)
    ]
    if len(branches) == 1:
        block_output, input_grad, w_in_grad, w_out_grad = branches[0](*args)
    else:
        block_output, input_grad, w_in_grad, w_out_grad = lax.switch(case, branches, *args)
    return (
        block_output.reshape(1, tl, width),
        input_grad.reshape(1, tl, width),
        w_in_grad,
        w_out_grad,
    )


def solution(mesh):
    placed = (
        P("rep", "col", "row"),
        P("row", ("rep", "col")),
        P(("rep", "col"), "row"),
        P("rep", "col", "row"),
        P(),
    )
    return jax.shard_map(
        body,
        mesh=mesh,
        in_specs=placed,
        out_specs=(
            P("rep", "col", "row"),
            P("rep", "col", "row"),
            P("row", ("rep", "col")),
            P(("rep", "col"), "row"),
        ),
        check_vma=False,
    )
```
